32 devices in a mesh: dp: 8 (over z, y), mp: 4 (over x, core).
Axes of the slice: x: 2, y: 2, z: 4, core: 2. Of those that a mesh axis runs over, the one named last changes fastest.
Arguments:
- hidden: bfloat16 [4096, 8192], P('dp', 'mp'), may hold values from -64 to 64
- queries: bfloat16 [4096, 4096], P('dp', 'mp'), may hold values from -512 to 512
- upstream: bfloat16 [4096, 4096], P('dp', 'mp'), may hold values from -6 to 6
- key_weight: bfloat16 [8192, 512], P(None, 'mp'), may hold values from -1 to 1
- value_weight: bfloat16 [8192, 512], P(None, 'mp'), may hold values from -0.0625 to 0.0625
- lengths: int32 [8, 8], replicated, may hold values from 0 to 64, as said below
- advantage: float32 [8, 8], replicated, may hold values from -4 to 4
Outputs:
- attention_out: bfloat16 [2048, 4096], P('dp', 'mp')
- key_grad: float32 [8192, 512], P('dp', 'mp')
- value_grad: float32 [8192, 512], P('dp', 'mp')
The draws below stay inside these ranges and needn't reach their ends.
Inputs may be any that keep to these rules, and one draw needn't show every extreme that they name: `lengths`: each rollout device fills its slots from slot 0; a used slot holds 33 to 64 tokens, later slots hold 0. Devices come in aligned groups of four; in each, the second or the third device is heavy and uses 6 to 8 slots; every other device uses one slot plus one for each neighbour that exists and is not heavy. One device's responses total at most 512 tokens and some device holds exactly 512; under the learner rule a learner receives at most 256 tokens and some learner exactly 256, and at most 128 tokens go from one device to one neighbour, exactly 128 from some device.
All inputs are finite; a program needn't handle non-finite values.
Results may differ from the reference program's by a relative error of at most 0.0082.
Values may be sent and summed in bfloat16 or wider, within the bound.
A program may use at most 128 MiB of HBM per device.

```python
import math
import jax
import jax.numpy as jnp
from jax import lax

D = 8192
QH = 32
KVH = 4
HD = 128
RESP = 8
LMAX = 64
CAP_R = 512
CAP_L = 256
ROWS_R = 4096
ROWS_L = 2048
N_DP = 8


def draw_lengths(key, part):
    base = jax.random.fold_in(key, 11)
    streams = jax.random.split(base, 6)
    device_total = ROWS_L // CAP_L
    group_total = device_total // 4
    heavy_place = jax.random.randint(streams[0], (group_total,), 1, 3)
    group_ids = jnp.arange(group_total)
    heavy_place = jnp.where(group_ids == 0, 2, jnp.where(group_ids == group_total - 1, 1, heavy_place))
    extra_count = jax.random.randint(streams[1], (group_total,), 2, 5)
    full_group = jax.random.randint(streams[4], (), 0, group_total)
    drawn = jax.random.randint(streams[5], (device_total, RESP), LMAX // 2 + 1, LMAX + 1)
    devices = jnp.arange(device_total)
    groups = devices // 4
    places = devices % 4
    heavy_flag = places == heavy_place[groups]
    forced = groups == full_group
    left_heavy = jnp.concatenate([jnp.zeros((1,), bool), heavy_flag[:-1]])
    right_heavy = jnp.concatenate([heavy_flag[1:], jnp.zeros((1,), bool)])
    has_left = devices > 0
    has_right = devices < device_total - 1
    light_left = (has_left & jnp.logical_not(left_heavy)).astype(jnp.int32)
    light_right = (has_right & jnp.logical_not(right_heavy)).astype(jnp.int32)
    extra_here = jnp.where(forced, 4, extra_count[groups])
    used_slots = jnp.where(heavy_flag, 4 + extra_here, 1 + light_left + light_right)
    slot_ids = jnp.arange(RESP)[None, :]
    drawn = jnp.where((heavy_flag & forced)[:, None], LMAX, drawn)
    lengths = jnp.where(slot_ids < used_slots[:, None], drawn, 0)
    return lengths.astype(jnp.int32)


def align_tables(key):
    base = jax.random.fold_in(key, 23)
    streams = jax.random.split(base, 4)
    weight = jnp.clip(jax.random.normal(streams[3], (D, KVH * HD), jnp.float32), -3.0, 3.0) * D ** (-0.5)
    return weight


def draw_key_weight(key, part):
    weight = align_tables(key)
    return weight.astype(jnp.bfloat16)


def draw_queries(key, part):
    streams = jax.random.split(jax.random.fold_in(key, 31), 1)
    values = jnp.clip(jax.random.normal(streams[0], (ROWS_R, QH * HD), jnp.float32), -6.0, 6.0)
    return values.astype(jnp.bfloat16)


def draw_hidden(key, part):
    streams = jax.random.split(jax.random.fold_in(key, 41), 3)
    row_scale = jnp.exp(jax.random.uniform(streams[0], (ROWS_R, 1), jnp.float32) * math.log(10.0))
    column_scale = jnp.exp(jax.random.uniform(streams[1], (1, D), jnp.float32) * math.log(10.0))
    noise = jnp.clip(jax.random.normal(streams[2], (ROWS_R, D), jnp.float32), -6.0, 6.0)
    values = noise * row_scale * column_scale * 0.1
    return values.astype(jnp.bfloat16)


def block_levels(stream_key, extent, shards, low, high):
    gain = 1.0
    for position, blocks in shards:
        draws = jax.random.uniform(jax.random.fold_in(jax.random.fold_in(stream_key, 6), position), (blocks,), jnp.float32, low / len(shards), high / len(shards))
        gain = gain * jnp.repeat(jnp.exp(draws), extent[position] // blocks).reshape((-1,) + (1,) * (len(extent) - 1 - position))
    return gain


def centred(key, shape, scale, limit, cuts=(), kind=jnp.bfloat16):
    array = jax.random.normal(key, shape, jnp.float32) * scale
    if len(cuts) > 0:
        array = block_levels(key, shape, cuts, -0.22, 0.18) * array
    return jnp.clip(array, min=-limit, max=limit).astype(kind)


def setup_inputs(seed: int = 0) -> dict:
    seeds = jax.random.split(jax.random.key(seed), 8)
    hidden = draw_hidden(jax.random.fold_in(seeds[7], 71), 0)
    queries = draw_queries(jax.random.fold_in(seeds[7], 71), 0)
    upstream = centred(seeds[2], (ROWS_R, QH * HD), 1.0, 6.0, ((0, 8), (1, 4)))
    key_weight = draw_key_weight(jax.random.fold_in(seeds[7], 71), 0)
    value_weight = centred(seeds[4], (D, KVH * HD), D ** -0.5, 0.0625, ((1, 4),))
    lengths = draw_lengths(jax.random.fold_in(seeds[7], 71), 0)
    advantage = centred(seeds[6], (N_DP, RESP), 1.0, 4.0, (), jnp.float32)
    return dict(hidden=hidden, queries=queries, upstream=upstream, key_weight=key_weight, value_weight=value_weight, lengths=lengths, advantage=advantage)


epsilon = 1e-06
masked_score = -1e+30

def derive_learner(lengths):
    device_total = lengths.shape[0]
    slot_total = lengths.shape[1]
    used_slots = lax.optimization_barrier(jnp.sum((lengths > 0).astype(jnp.int32), axis=1)).astype(jnp.int32)
    heavy_flag = used_slots >= 6
    devices = jnp.arange(device_total, dtype=jnp.int32)
    left_heavy = jnp.concatenate([jnp.zeros((1,), bool), heavy_flag[:-1]])
    light_left = ((devices > 0) & jnp.logical_not(left_heavy)).astype(jnp.int32)
    sent_left = jnp.where(heavy_flag, (used_slots - 4) // 2, light_left).astype(jnp.int32)
    kept_count = jnp.where(heavy_flag, 4, 1).astype(jnp.int32)
    slot_ids = jnp.arange(slot_total, dtype=jnp.int32)[None, :]
    slot_moves = jnp.where(slot_ids < sent_left[:, None], -1, jnp.where(slot_ids < (sent_left + kept_count)[:, None], 0, jnp.where(slot_ids < used_slots[:, None], 1, 0)))
    return (devices[:, None] + slot_moves).astype(jnp.int32)

def normalize_rows(values):
    widened = values.astype(jnp.float32)
    scale = lax.rsqrt(lax.optimization_barrier(jnp.mean(widened * widened, axis=-1, keepdims=True)) + epsilon)
    return (widened * scale).astype(jnp.bfloat16)

def settle(values):
    return lax.optimization_barrier(values.astype(jnp.bfloat16)).astype(jnp.float32)

def reference(hidden, queries, upstream, key_weight, value_weight, lengths, advantage):
    device_total = lengths.shape[0]
    slot_total = lengths.shape[1]
    group_size = QH // KVH
    inverse_root = HD ** (-0.5)
    offsets = jnp.arange(LMAX, dtype=jnp.int32)
    row_ids = jnp.arange(CAP_R, dtype=jnp.int32)
    learner = derive_learner(lengths)

    def one_device(carry, device):
        key_acc, value_acc = carry
        first_row = (device * CAP_R).astype(jnp.int32)
        hidden_rows = lax.dynamic_slice_in_dim(hidden, first_row, CAP_R, 0)
        query_rows = lax.dynamic_slice_in_dim(queries, first_row, CAP_R, 0)
        upstream_rows = lax.dynamic_slice_in_dim(upstream, first_row, CAP_R, 0)
        normed = normalize_rows(hidden_rows)
        key_rows = jnp.dot(normed, key_weight, preferred_element_type=jnp.float32).astype(jnp.bfloat16)
        value_rows = jnp.dot(normed, value_weight, preferred_element_type=jnp.float32).astype(jnp.bfloat16)
        slot_lengths = lengths[device].astype(jnp.int32)
        slot_ends = jnp.cumsum(slot_lengths).astype(jnp.int32)
        slot_starts = (slot_ends - slot_lengths).astype(jnp.int32)
        window = jnp.clip(slot_starts[:, None] + offsets[None, :], 0, CAP_R - 1).astype(jnp.int32)
        inside = offsets[None, :] < slot_lengths[:, None]
        rates = advantage[device] / jnp.maximum(slot_lengths, 1).astype(jnp.float32)
        normed_window = normed[window]
        query_window = query_rows[window].astype(jnp.float32).reshape(slot_total, LMAX, KVH, group_size, HD)
        key_window = key_rows[window].astype(jnp.float32).reshape(slot_total, LMAX, KVH, HD)
        value_window = value_rows[window].astype(jnp.float32).reshape(slot_total, LMAX, KVH, HD)
        cot_window = jnp.where(inside[:, :, None], rates[:, None, None] * upstream_rows[window].astype(jnp.float32), 0.0)
        cot_window = settle(cot_window).reshape(slot_total, LMAX, KVH, group_size, HD)
        allowed = (offsets[None, :] <= offsets[:, None])[None, :, :] & inside[:, None, :]
        scores = jnp.einsum('rtkgd,rukd->rkgtu', query_window, key_window) * inverse_root
        scores = jnp.where(allowed[:, None, None, :, :], scores, masked_score)
        row_peak = lax.optimization_barrier(jnp.max(scores, axis=-1, keepdims=True))
        raised = jnp.exp(scores - row_peak)
        probability = raised / lax.optimization_barrier(jnp.sum(raised, axis=-1, keepdims=True))
        weights = settle(probability)
        attended = jnp.einsum('rkgtu,rukd->rtkgd', weights, value_window).astype(jnp.bfloat16)
        prob_grad = jnp.einsum('rtkgd,rukd->rkgtu', cot_window, value_window)
        centre = lax.optimization_barrier(jnp.sum(probability * prob_grad, axis=-1, keepdims=True))
        score_grad = settle(probability * (prob_grad - centre))
        key_cot = (jnp.einsum('rkgtu,rtkgd->rukd', score_grad, query_window) * inverse_root).astype(jnp.bfloat16)
        value_cot = jnp.einsum('rkgtu,rtkgd->rukd', weights, cot_window).astype(jnp.bfloat16)
        flat_normed = normed_window.reshape(slot_total * LMAX, D)
        key_acc = key_acc + jnp.dot(flat_normed.T, key_cot.reshape(slot_total * LMAX, KVH * HD), preferred_element_type=jnp.float32)
        value_acc = value_acc + jnp.dot(flat_normed.T, value_cot.reshape(slot_total * LMAX, KVH * HD), preferred_element_type=jnp.float32)
        slot_of_row = jnp.minimum(lax.optimization_barrier(jnp.sum((row_ids[:, None] >= slot_ends[None, :]).astype(jnp.int32), axis=1)), slot_total - 1).astype(jnp.int32)
        offset_of_row = jnp.clip(row_ids - slot_starts[slot_of_row], 0, LMAX - 1).astype(jnp.int32)
        attended_rows = attended.reshape(slot_total * LMAX, QH * HD)[slot_of_row * LMAX + offset_of_row]
        return ((key_acc, value_acc), attended_rows)
    empty = jnp.zeros((D, KVH * HD), jnp.float32)
    (key_grad, value_grad), attended_all = lax.scan(one_device, (empty, empty), jnp.arange(device_total, dtype=jnp.int32))
    attended_flat = attended_all.reshape(device_total * CAP_R, QH * HD)
    flat_lengths = lengths.reshape(-1).astype(jnp.int32)
    flat_dest = learner.reshape(-1).astype(jnp.int32)
    dest_hits = (flat_dest[:, None] == jnp.arange(device_total, dtype=jnp.int32)[None, :]).astype(jnp.int32)
    lane_tokens = dest_hits * flat_lengths[:, None]
    before = (jnp.cumsum(lane_tokens, axis=0).astype(jnp.int32) - lane_tokens).astype(jnp.int32)
    learner_start = lax.optimization_barrier(jnp.sum(before * dest_hits, axis=1)).astype(jnp.int32)
    all_ends = jnp.cumsum(lengths.astype(jnp.int32), axis=1).astype(jnp.int32)
    device_base = (jnp.arange(device_total, dtype=jnp.int32) * CAP_R).astype(jnp.int32)
    rollout_start = (device_base[:, None] + all_ends - lengths.astype(jnp.int32)).reshape(-1).astype(jnp.int32)
    learner_rows = jnp.arange(device_total * CAP_L, dtype=jnp.int32)
    target = (learner_rows // CAP_L).astype(jnp.int32)
    within = (learner_rows % CAP_L).astype(jnp.int32)
    hits = (flat_dest[None, :] == target[:, None]) & (learner_start[None, :] <= within[:, None]) & (within[:, None] < learner_start[None, :] + flat_lengths[None, :])
    source = lax.optimization_barrier(jnp.sum(jnp.where(hits, rollout_start[None, :] + within[:, None] - learner_start[None, :], 0), axis=1)).astype(jnp.int32)
    filled = jnp.any(hits, axis=1)
    attention_out = jnp.where(filled[:, None], attended_flat[source], jnp.zeros((), jnp.bfloat16))
    return (attention_out, key_grad, value_grad)
```

```python
import jax
import jax.numpy as jnp
from jax import lax
from jax.experimental import pallas as pl
from jax.experimental.pallas import tpu as pltpu
from jax.sharding import PartitionSpec as P

HD = 128
CAP_R = 512
CAP_L = 256
PIECE = 128
LAST_START = CAP_R - PIECE

epsilon = 1e-06
masked_score = -1e30


def passed_along(value, axis, steps):
    count = lax.axis_size(axis)
    first, last = (max(0, -steps), min(count, count - steps))
    return lax.ppermute(value, axis, [(source, source + steps) for source in range(first, last)])


def derive_moves(lengths):
    device_total, slot_total = lengths.shape
    used_slots = jnp.sum((lengths > 0).astype(jnp.int32), axis=1)
    heavy_flag = used_slots >= 6
    devices = jnp.arange(device_total, dtype=jnp.int32)
    left_heavy = jnp.concatenate([jnp.zeros((1,), bool), heavy_flag[:-1]])
    light_left = ((devices > 0) & jnp.logical_not(left_heavy)).astype(jnp.int32)
    sent_left = jnp.where(heavy_flag, (used_slots - 4) // 2, light_left)
    kept_count = jnp.where(heavy_flag, 4, 1).astype(jnp.int32)
    slot_ids = jnp.arange(slot_total, dtype=jnp.int32)[None, :]
    return jnp.where(
        slot_ids < sent_left[:, None],
        -1,
        jnp.where(
            slot_ids < (sent_left + kept_count)[:, None],
            0,
            jnp.where(slot_ids < used_slots[:, None], 1, 0),
        ),
    )


def learner_rows(lengths, advantage, device):
    device_total, slot_total = lengths.shape
    moves = derive_moves(lengths)
    slot_ids = jnp.arange(slot_total, dtype=jnp.int32)
    before = (slot_ids[:, None] < slot_ids[None, :]).astype(jnp.int32)
    begins = jnp.sum(lengths[:, :, None] * before[None], axis=1)
    piece_start = jnp.minimum(jnp.sum(jnp.where(moves < 1, lengths, 0), axis=1), LAST_START)
    bases = jnp.stack(
        [begins - piece_start[:, None], begins + PIECE, begins + PIECE + CAP_R], axis=0
    )
    table = jnp.pad(lengths, ((1, 1), (0, 0)))
    window = lax.dynamic_slice_in_dim(table, device, 3, 0)
    move_window = lax.dynamic_slice_in_dim(jnp.pad(moves, ((1, 1), (0, 0))), device, 3, 0)
    rate_window = lax.dynamic_slice_in_dim(jnp.pad(advantage, ((1, 1), (0, 0))), device, 3, 0)
    base_window = lax.dynamic_slice_in_dim(jnp.pad(bases, ((0, 0), (1, 1), (0, 0))), device, 3, 1)
    base_window = jnp.stack([base_window[0, 0], base_window[1, 1], base_window[2, 2]], axis=0)
    wanted = jnp.array([1, 0, -1], jnp.int32)[:, None]
    sizes = jnp.where(move_window == wanted, window, 0).reshape(-1)
    rates = rate_window.reshape(-1) / jnp.maximum(sizes, 1).astype(jnp.float32)
    places = base_window.reshape(-1)
    ids = jnp.arange(3 * slot_total, dtype=jnp.int32)
    starts = jnp.sum(jnp.where(ids[:, None] < ids[None, :], sizes[:, None], 0), axis=0)
    ends = starts + sizes
    rows = jnp.arange(CAP_L, dtype=jnp.int32)
    hits = (rows[:, None] >= starts[None, :]) & (rows[:, None] < ends[None, :])
    segments = jnp.sum((rows[:, None] >= ends[None, :]).astype(jnp.int32), axis=1)
    scales = jnp.sum(jnp.where(hits, rates[None, :], 0.0), axis=1)
    source = jnp.sum(jnp.where(hits, (places - starts)[None, :] + rows[:, None] + 1, 0), axis=1) - 1
    own_piece = lax.dynamic_index_in_dim(piece_start, device, 0, keepdims=False)
    return segments, scales, source, own_piece


def attention_kernel(q_ref, k_ref, v_ref, u_ref, scale_ref, seg_col_ref, seg_row_ref,
                     out_ref, cots_ref, key_acc, value_acc):
    head = pl.program_id(0)
    inverse_root = HD ** (-0.5)
    rows = q_ref.shape[0]
    query, key, value = q_ref[...], k_ref[...], v_ref[...]
    cot = (scale_ref[...] * u_ref[...].astype(jnp.float32)).astype(jnp.bfloat16)
    t = lax.broadcasted_iota(jnp.int32, (rows, rows), 0)
    u = lax.broadcasted_iota(jnp.int32, (rows, rows), 1)
    allowed = (u <= t) & (seg_col_ref[...] == seg_row_ref[...])
    across = (((1,), (1,)), ((), ()))
    down = (((0,), (0,)), ((), ()))
    scores = lax.dot_general(query, key, across, preferred_element_type=jnp.float32) * inverse_root
    scores = jnp.where(allowed, scores, masked_score)
    raised = jnp.exp(scores - jnp.max(scores, axis=-1, keepdims=True))
    probability = raised * (1.0 / jnp.sum(raised, axis=-1, keepdims=True))
    weights = probability.astype(jnp.bfloat16)
    out_ref[...] = jnp.dot(weights, value, preferred_element_type=jnp.float32).astype(jnp.bfloat16)
    prob_grad = lax.dot_general(cot, value, across, preferred_element_type=jnp.float32)
    centre = jnp.sum(probability * prob_grad, axis=-1, keepdims=True)
    score_grad = (probability * (prob_grad - centre)).astype(jnp.bfloat16)
    key_term = lax.dot_general(score_grad, query, down, preferred_element_type=jnp.float32)
    value_term = lax.dot_general(weights, cot, down, preferred_element_type=jnp.float32)

    @pl.when(head == 0)
    def _():
        key_acc[...] = key_term
        value_acc[...] = value_term

    @pl.when(head > 0)
    def _():
        key_acc[...] += key_term
        value_acc[...] += value_term

    @pl.when(head == pl.num_programs(0) - 1)
    def _():
        cots_ref[:, :HD] = (key_acc[...] * inverse_root).astype(jnp.bfloat16)
        cots_ref[:, HD:] = value_acc[...].astype(jnp.bfloat16)


def attend(queries, keys_values, upstream, scales, segments):
    rows, width = queries.shape
    head_block = pl.BlockSpec((rows, HD), lambda h: (0, h))
    whole = lambda shape: pl.BlockSpec(shape, lambda h: (0, 0))
    return pl.pallas_call(
        attention_kernel,
        grid=(width // HD,),
        in_specs=[
            head_block,
            pl.BlockSpec((rows, HD), lambda h: (0, 0)),
            pl.BlockSpec((rows, HD), lambda h: (0, 1)),
            head_block,
            whole((rows, 1)),
            whole((rows, 1)),
            whole((1, rows)),
        ],
        out_specs=[head_block, whole((rows, 2 * HD))],
        out_shape=[
            jax.ShapeDtypeStruct((rows, width), jnp.bfloat16),
            jax.ShapeDtypeStruct((rows, 2 * HD), jnp.bfloat16),
        ],
        scratch_shapes=[pltpu.VMEM((rows, HD), jnp.float32), pltpu.VMEM((rows, HD), jnp.float32)],
        compiler_params=pltpu.CompilerParams(dimension_semantics=("arbitrary",)),
    )(queries, keys_values, keys_values, upstream, scales[:, None], segments[:, None], segments[None, :])


def body(hidden, queries, upstream, key_weight, value_weight, lengths, advantage):
    device = lax.axis_index("dp")
    segments, scales, source, own_piece = learner_rows(lengths, advantage, device)
    positions = jnp.arange(2 * PIECE + CAP_R, dtype=jnp.int32)
    pick = (source[:, None] == positions[None, :]).astype(jnp.bfloat16)

    def exchanged(array):
        later = lax.dynamic_slice_in_dim(array, own_piece, PIECE, 0)
        return passed_along(later, "dp", 1), passed_along(array[:PIECE], "dp", -1)

    def settled(array, pieces):
        pool = jnp.concatenate([pieces[0], array, pieces[1]], axis=0)
        return jnp.dot(pick, pool, preferred_element_type=jnp.float32).astype(jnp.bfloat16)

    hidden_pieces = exchanged(hidden)
    query_pieces = exchanged(queries)
    upstream_pieces = exchanged(upstream)
    full = lax.all_gather(settled(hidden, hidden_pieces), "mp", axis=1, tiled=True)
    query_rows = settled(queries, query_pieces)
    upstream_rows = settled(upstream, upstream_pieces)
    weight = jnp.concatenate([key_weight, value_weight], axis=1)
    widened = full.astype(jnp.float32)
    normed = (
        widened * lax.rsqrt(jnp.mean(widened * widened, axis=1, keepdims=True) + epsilon)
    ).astype(jnp.bfloat16)
    keys_values = jnp.dot(normed, weight, preferred_element_type=jnp.float32).astype(jnp.bfloat16)
    attention_out, cots = attend(query_rows, keys_values, upstream_rows, scales, segments)
    term = lax.dot_general(
        normed, cots, (((0,), (0,)), ((), ())), preferred_element_type=jnp.float32
    ).astype(jnp.bfloat16)
    summed = lax.psum_scatter(term, "dp", scatter_dimension=0, tiled=True).astype(jnp.float32)
    return (attention_out, summed[:, :HD], summed[:, HD:])


def solution(mesh):
    in_specs = (P("dp", "mp"), P("dp", "mp"), P("dp", "mp"), P(None, "mp"), P(None, "mp"), P(), P())
    out_specs = (P("dp", "mp"), P("dp", "mp"), P("dp", "mp"))
    return jax.shard_map(body, mesh=mesh, in_specs=in_specs, out_specs=out_specs, check_vma=False)
```

```python
import functools

import jax
import jax.numpy as jnp
from jax import lax
from jax.experimental import pallas as pl
from jax.experimental.pallas import tpu as pltpu
from jax.sharding import PartitionSpec as P

HD = 128
CAP_R = 512
CAP_L = 256
PIECE = 128
LAST_START = CAP_R - PIECE

epsilon = 1e-06
masked_score = -1e30


def passed_along(value, axis, steps):
    count = lax.axis_size(axis)
    first, last = (max(0, -steps), min(count, count - steps))
    return lax.ppermute(value, axis, [(source, source + steps) for source in range(first, last)])


def derive_moves(lengths):
    device_total, slot_total = lengths.shape
    used_slots = jnp.sum((lengths > 0).astype(jnp.int32), axis=1)
    heavy_flag = used_slots >= 6
    devices = jnp.arange(device_total, dtype=jnp.int32)
    left_heavy = jnp.concatenate([jnp.zeros((1,), bool), heavy_flag[:-1]])
    light_left = ((devices > 0) & jnp.logical_not(left_heavy)).astype(jnp.int32)
    sent_left = jnp.where(heavy_flag, (used_slots - 4) // 2, light_left)
    kept_count = jnp.where(heavy_flag, 4, 1).astype(jnp.int32)
    slot_ids = jnp.arange(slot_total, dtype=jnp.int32)[None, :]
    return jnp.where(
        slot_ids < sent_left[:, None],
        -1,
        jnp.where(
            slot_ids < (sent_left + kept_count)[:, None],
            0,
            jnp.where(slot_ids < used_slots[:, None], 1, 0),
        ),
    )


def learner_rows(lengths, advantage, device):
    device_total, slot_total = lengths.shape
    moves = derive_moves(lengths)
    slot_ids = jnp.arange(slot_total, dtype=jnp.int32)
    before = (slot_ids[:, None] < slot_ids[None, :]).astype(jnp.int32)
    begins = jnp.sum(lengths[:, :, None] * before[None], axis=1)
    piece_start = jnp.minimum(jnp.sum(jnp.where(moves < 1, lengths, 0), axis=1), LAST_START)
    bases = jnp.stack(
        [begins - piece_start[:, None], begins + PIECE, begins + PIECE + CAP_R], axis=0
    )
    table = jnp.pad(lengths, ((1, 1), (0, 0)))
    window = lax.dynamic_slice_in_dim(table, device, 3, 0)
    move_window = lax.dynamic_slice_in_dim(jnp.pad(moves, ((1, 1), (0, 0))), device, 3, 0)
    rate_window = lax.dynamic_slice_in_dim(jnp.pad(advantage, ((1, 1), (0, 0))), device, 3, 0)
    base_window = lax.dynamic_slice_in_dim(jnp.pad(bases, ((0, 0), (1, 1), (0, 0))), device, 3, 1)
    base_window = jnp.stack([base_window[0, 0], base_window[1, 1], base_window[2, 2]], axis=0)
    wanted = jnp.array([1, 0, -1], jnp.int32)[:, None]
    sizes = jnp.where(move_window == wanted, window, 0).reshape(-1)
    rates = rate_window.reshape(-1) / jnp.maximum(sizes, 1).astype(jnp.float32)
    places = base_window.reshape(-1)
    ids = jnp.arange(3 * slot_total, dtype=jnp.int32)
    starts = jnp.sum(jnp.where(ids[:, None] < ids[None, :], sizes[:, None], 0), axis=0)
    ends = starts + sizes
    rows = jnp.arange(CAP_L, dtype=jnp.int32)
    hits = (rows[:, None] >= starts[None, :]) & (rows[:, None] < ends[None, :])
    segments = jnp.sum((rows[:, None] >= ends[None, :]).astype(jnp.int32), axis=1)
    scales = jnp.sum(jnp.where(hits, rates[None, :], 0.0), axis=1)
    source = jnp.sum(jnp.where(hits, (places - starts)[None, :] + rows[:, None] + 1, 0), axis=1) - 1
    own_piece = lax.dynamic_index_in_dim(piece_start, device, 0, keepdims=False)
    return segments, scales, source, own_piece


def attention_kernel(q_ref, k_ref, v_ref, u_ref, scale_ref, seg_col_ref, seg_row_ref,
                     out_ref, cots_ref, key_acc, value_acc):
    head = pl.program_id(0)
    inverse_root = HD ** (-0.5)
    rows = q_ref.shape[0]
    query, key, value = q_ref[...], k_ref[...], v_ref[...]
    cot = (scale_ref[...] * u_ref[...].astype(jnp.float32)).astype(jnp.bfloat16)
    t = lax.broadcasted_iota(jnp.int32, (rows, rows), 0)
    u = lax.broadcasted_iota(jnp.int32, (rows, rows), 1)
    allowed = (u <= t) & (seg_col_ref[...] == seg_row_ref[...])
    across = (((1,), (1,)), ((), ()))
    down = (((0,), (0,)), ((), ()))
    scores = lax.dot_general(query, key, across, preferred_element_type=jnp.float32) * inverse_root
    scores = jnp.where(allowed, scores, masked_score)
    raised = jnp.exp(scores - jnp.max(scores, axis=-1, keepdims=True))
    probability = raised * (1.0 / jnp.sum(raised, axis=-1, keepdims=True))
    weights = probability.astype(jnp.bfloat16)
    out_ref[...] = jnp.dot(weights, value, preferred_element_type=jnp.float32).astype(jnp.bfloat16)
    prob_grad = lax.dot_general(cot, value, across, preferred_element_type=jnp.float32)
    centre = jnp.sum(probability * prob_grad, axis=-1, keepdims=True)
    score_grad = (probability * (prob_grad - centre)).astype(jnp.bfloat16)
    key_term = lax.dot_general(query, score_grad, down, preferred_element_type=jnp.float32)
    value_term = lax.dot_general(cot, weights, down, preferred_element_type=jnp.float32)

    @pl.when(head == 0)
    def _():
        key_acc[...] = key_term
        value_acc[...] = value_term

    @pl.when(head > 0)
    def _():
        key_acc[...] += key_term
        value_acc[...] += value_term

    @pl.when(head == pl.num_programs(0) - 1)
    def _():
        cots_ref[:HD] = (key_acc[...] * inverse_root).astype(jnp.bfloat16)
        cots_ref[HD:] = value_acc[...].astype(jnp.bfloat16)


def attend(queries, keys_values, upstream, scales, segments):
    rows, width = queries.shape
    head_block = pl.BlockSpec((rows, HD), lambda h: (0, h))
    whole = lambda shape: pl.BlockSpec(shape, lambda h: (0, 0))
    return pl.pallas_call(
        attention_kernel,
        grid=(width // HD,),
        in_specs=[
            head_block,
            pl.BlockSpec((rows, HD), lambda h: (0, 0)),
            pl.BlockSpec((rows, HD), lambda h: (0, 1)),
            head_block,
            whole((rows, 1)),
            whole((rows, 1)),
            whole((1, rows)),
        ],
        out_specs=[head_block, whole((2 * HD, rows))],
        out_shape=[
            jax.ShapeDtypeStruct((rows, width), jnp.bfloat16),
            jax.ShapeDtypeStruct((2 * HD, rows), jnp.bfloat16),
        ],
        scratch_shapes=[pltpu.VMEM((HD, rows), jnp.float32), pltpu.VMEM((HD, rows), jnp.float32)],
        compiler_params=pltpu.CompilerParams(dimension_semantics=("arbitrary",)),
    )(queries, keys_values, keys_values, upstream, scales[:, None], segments[:, None], segments[None, :])


def gradient_kernel(count, normed_ref, cots_ref, key_ref, value_ref, pair_out, pair_in, line_out,
                    line_in, acc, pair_sent, pair_got, line_sent, line_got):
    me = lax.axis_index("dp")
    lines = count // 2
    line, side = me // 2, me % 2
    width = acc.shape[1]
    mesh_id = pl.DeviceIdType.MESH

    def place(k):
        return (line + 1 + k) % lines

    def share(owner):
        columns = pl.ds(pl.multiple_of(owner * width, width), width)
        return jnp.dot(cots_ref[...], normed_ref[:, columns], preferred_element_type=jnp.float32)

    def pair_copy(k):
        return pltpu.make_async_remote_copy(
            src_ref=pair_out.at[k], dst_ref=pair_in.at[k],
            send_sem=pair_sent.at[k], recv_sem=pair_got.at[k],
            device_id={"dp": line * 2 + 1 - side}, device_id_type=mesh_id,
        )

    def line_copy(k):
        return pltpu.make_async_remote_copy(
            src_ref=line_out.at[k], dst_ref=line_in.at[k],
            send_sem=line_sent.at[k], recv_sem=line_got.at[k],
            device_id={"dp": place(k) * 2 + side}, device_id_type=mesh_id,
        )

    barrier = pltpu.get_barrier_semaphore()
    pl.semaphore_signal(barrier, inc=1, device_id={"dp": line * 2 + 1 - side}, device_id_type=mesh_id)

    @pl.loop(0, lines - 1)
    def _(k):
        pl.semaphore_signal(barrier, inc=1, device_id={"dp": place(k) * 2 + side}, device_id_type=mesh_id)

    pl.semaphore_wait(barrier, lines)

    @pl.loop(0, lines)
    def _(k):
        pair_out[k] = share(place(k) * 2 + 1 - side).astype(jnp.bfloat16)
        pair_copy(k).start()

    @pl.loop(0, lines - 1)
    def _(k):
        own = share(place(k) * 2 + side)
        pair_copy(k).wait_recv()
        line_out[k] = (own + pair_in[k].astype(jnp.float32)).astype(jnp.bfloat16)
        line_copy(k).start()

    acc[...] = share(me)
    pair_copy(lines - 1).wait_recv()
    acc[...] += pair_in[lines - 1].astype(jnp.float32)

    @pl.loop(0, lines - 1)
    def _(k):
        line_copy(k).wait_recv()
        acc[...] += line_in[k].astype(jnp.float32)

    key_ref[...] = acc[:HD].T
    value_ref[...] = acc[HD:].T

    @pl.loop(0, lines)
    def _(k):
        pair_copy(k).wait_send()

    @pl.loop(0, lines - 1)
    def _(k):
        line_copy(k).wait_send()


def gradient_sum(normed, cots):
    count = lax.axis_size("dp")
    lines = count // 2
    width = normed.shape[1] // count
    vmem = pl.BlockSpec(memory_space=pltpu.VMEM)
    shares = lambda n: pltpu.VMEM((n, 2 * HD, width), jnp.bfloat16)
    return pl.pallas_call(
        functools.partial(gradient_kernel, count),
        in_specs=[vmem, vmem],
        out_specs=[vmem, vmem],
        out_shape=[jax.ShapeDtypeStruct((width, HD), jnp.float32)] * 2,
        scratch_shapes=[
            shares(lines),
            shares(lines),
            shares(lines - 1),
            shares(lines - 1),
            pltpu.VMEM((2 * HD, width), jnp.float32),
            pltpu.SemaphoreType.DMA((lines,)),
            pltpu.SemaphoreType.DMA((lines,)),
            pltpu.SemaphoreType.DMA((lines - 1,)),
            pltpu.SemaphoreType.DMA((lines - 1,)),
        ],
        compiler_params=pltpu.CompilerParams(
            collective_id=0, has_side_effects=True, vmem_limit_bytes=40 * 1024 * 1024
        ),
    )(normed, cots)


def body(hidden, queries, upstream, key_weight, value_weight, lengths, advantage):
    device = lax.axis_index("dp")
    segments, scales, source, own_piece = learner_rows(lengths, advantage, device)
    positions = jnp.arange(2 * PIECE + CAP_R, dtype=jnp.int32)
    pick = (source[:, None] == positions[None, :]).astype(jnp.bfloat16)

    def exchanged(array):
        later = lax.dynamic_slice_in_dim(array, own_piece, PIECE, 0)
        return passed_along(later, "dp", 1), passed_along(array[:PIECE], "dp", -1)

    def settled(array, pieces):
        pool = jnp.concatenate([pieces[0], array, pieces[1]], axis=0)
        return jnp.dot(pick, pool, preferred_element_type=jnp.float32).astype(jnp.bfloat16)

    hidden_pieces = exchanged(hidden)
    query_pieces = exchanged(queries)
    upstream_pieces = exchanged(upstream)
    full = lax.all_gather(settled(hidden, hidden_pieces), "mp", axis=1, tiled=True)
    query_rows = settled(queries, query_pieces)
    upstream_rows = settled(upstream, upstream_pieces)
    weight = jnp.concatenate([key_weight, value_weight], axis=1)
    widened = full.astype(jnp.float32)
    normed = (
        widened * lax.rsqrt(jnp.mean(widened * widened, axis=1, keepdims=True) + epsilon)
    ).astype(jnp.bfloat16)
    keys_values = jnp.dot(normed, weight, preferred_element_type=jnp.float32).astype(jnp.bfloat16)
    attention_out, cots = attend(query_rows, keys_values, upstream_rows, scales, segments)
    key_grad, value_grad = gradient_sum(normed, cots)
    return (attention_out, key_grad, value_grad)


def solution(mesh):
    in_specs = (P("dp", "mp"), P("dp", "mp"), P("dp", "mp"), P(None, "mp"), P(None, "mp"), P(), P())
    out_specs = (P("dp", "mp"), P("dp", "mp"), P("dp", "mp"))
    return jax.shard_map(body, mesh=mesh, in_specs=in_specs, out_specs=out_specs, check_vma=False)
```

```python
import functools

import jax
import jax.numpy as jnp
from jax import lax
from jax.experimental import pallas as pl
from jax.experimental.pallas import tpu as pltpu
from jax.sharding import PartitionSpec as P

HD = 128
CAP_R = 512
CAP_L = 256
PIECE = 128
LAST_START = CAP_R - PIECE
CHUNKS = 4

epsilon = 1e-06
masked_score = -1e30


def derive_moves(lengths):
    device_total, slot_total = lengths.shape
    used_slots = jnp.sum((lengths > 0).astype(jnp.int32), axis=1)
    heavy_flag = used_slots >= 6
    devices = jnp.arange(device_total, dtype=jnp.int32)
    left_heavy = jnp.concatenate([jnp.zeros((1,), bool), heavy_flag[:-1]])
    light_left = ((devices > 0) & jnp.logical_not(left_heavy)).astype(jnp.int32)
    sent_left = jnp.where(heavy_flag, (used_slots - 4) // 2, light_left)
    kept_count = jnp.where(heavy_flag, 4, 1).astype(jnp.int32)
    slot_ids = jnp.arange(slot_total, dtype=jnp.int32)[None, :]
    return jnp.where(
        slot_ids < sent_left[:, None],
        -1,
        jnp.where(
            slot_ids < (sent_left + kept_count)[:, None],
            0,
            jnp.where(slot_ids < used_slots[:, None], 1, 0),
        ),
    )


def learner_rows(lengths, advantage, device):
    device_total, slot_total = lengths.shape
    moves = derive_moves(lengths)
    slot_ids = jnp.arange(slot_total, dtype=jnp.int32)
    before = (slot_ids[:, None] < slot_ids[None, :]).astype(jnp.int32)
    begins = jnp.sum(lengths[:, :, None] * before[None], axis=1)
    piece_start = jnp.minimum(jnp.sum(jnp.where(moves < 1, lengths, 0), axis=1), LAST_START)
    bases = jnp.stack(
        [begins - piece_start[:, None], begins + PIECE, begins + PIECE + CAP_R], axis=0
    )
    table = jnp.pad(lengths, ((1, 1), (0, 0)))
    window = lax.dynamic_slice_in_dim(table, device, 3, 0)
    move_window = lax.dynamic_slice_in_dim(jnp.pad(moves, ((1, 1), (0, 0))), device, 3, 0)
    rate_window = lax.dynamic_slice_in_dim(jnp.pad(advantage, ((1, 1), (0, 0))), device, 3, 0)
    base_window = lax.dynamic_slice_in_dim(jnp.pad(bases, ((0, 0), (1, 1), (0, 0))), device, 3, 1)
    base_window = jnp.stack([base_window[0, 0], base_window[1, 1], base_window[2, 2]], axis=0)
    wanted = jnp.array([1, 0, -1], jnp.int32)[:, None]
    sizes = jnp.where(move_window == wanted, window, 0).reshape(-1)
    rates = rate_window.reshape(-1) / jnp.maximum(sizes, 1).astype(jnp.float32)
    places = base_window.reshape(-1)
    ids = jnp.arange(3 * slot_total, dtype=jnp.int32)
    starts = jnp.sum(jnp.where(ids[:, None] < ids[None, :], sizes[:, None], 0), axis=0)
    ends = starts + sizes
    rows = jnp.arange(CAP_L, dtype=jnp.int32)
    hits = (rows[:, None] >= starts[None, :]) & (rows[:, None] < ends[None, :])
    segments = jnp.sum((rows[:, None] >= ends[None, :]).astype(jnp.int32), axis=1)
    scales = jnp.sum(jnp.where(hits, rates[None, :], 0.0), axis=1)
    source = jnp.sum(jnp.where(hits, (places - starts)[None, :] + rows[:, None] + 1, 0), axis=1) - 1
    own_piece = lax.dynamic_index_in_dim(piece_start, device, 0, keepdims=False)
    return segments, scales, source, own_piece


def attention_kernel(q_ref, k_ref, v_ref, u_ref, scale_ref, seg_col_ref, seg_row_ref,
                     out_ref, cots_ref, key_acc, value_acc):
    head = pl.program_id(0)
    inverse_root = HD ** (-0.5)
    rows = q_ref.shape[0]
    query, key, value = q_ref[...], k_ref[...], v_ref[...]
    cot = (scale_ref[...] * u_ref[...].astype(jnp.float32)).astype(jnp.bfloat16)
    t = lax.broadcasted_iota(jnp.int32, (rows, rows), 0)
    u = lax.broadcasted_iota(jnp.int32, (rows, rows), 1)
    allowed = (u <= t) & (seg_col_ref[...] == seg_row_ref[...])
    across = (((1,), (1,)), ((), ()))
    down = (((0,), (0,)), ((), ()))
    scores = lax.dot_general(query, key, across, preferred_element_type=jnp.float32) * inverse_root
    scores = jnp.where(allowed, scores, masked_score)
    raised = jnp.exp(scores - jnp.max(scores, axis=-1, keepdims=True))
    probability = raised * (1.0 / jnp.sum(raised, axis=-1, keepdims=True))
    weights = probability.astype(jnp.bfloat16)
    out_ref[...] = jnp.dot(weights, value, preferred_element_type=jnp.float32).astype(jnp.bfloat16)
    prob_grad = lax.dot_general(cot, value, across, preferred_element_type=jnp.float32)
    centre = jnp.sum(probability * prob_grad, axis=-1, keepdims=True)
    score_grad = (probability * (prob_grad - centre)).astype(jnp.bfloat16)
    key_term = lax.dot_general(query, score_grad, down, preferred_element_type=jnp.float32)
    value_term = lax.dot_general(cot, weights, down, preferred_element_type=jnp.float32)

    @pl.when(head == 0)
    def _():
        key_acc[...] = key_term
        value_acc[...] = value_term

    @pl.when(head > 0)
    def _():
        key_acc[...] += key_term
        value_acc[...] += value_term

    @pl.when(head == pl.num_programs(0) - 1)
    def _():
        cots_ref[:HD] = (key_acc[...] * inverse_root).astype(jnp.bfloat16)
        cots_ref[HD:] = value_acc[...].astype(jnp.bfloat16)


def attend(queries, keys_values, upstream, scales, segments):
    rows, width = queries.shape
    head_block = pl.BlockSpec((rows, HD), lambda h: (0, h))
    whole = lambda shape: pl.BlockSpec(shape, lambda h: (0, 0))
    return pl.pallas_call(
        attention_kernel,
        grid=(width // HD,),
        in_specs=[
            head_block,
            pl.BlockSpec((rows, HD), lambda h: (0, 0)),
            pl.BlockSpec((rows, HD), lambda h: (0, 1)),
            head_block,
            whole((rows, 1)),
            whole((rows, 1)),
            whole((1, rows)),
        ],
        out_specs=[head_block, whole((2 * HD, rows))],
        out_shape=[
            jax.ShapeDtypeStruct((rows, width), jnp.bfloat16),
            jax.ShapeDtypeStruct((2 * HD, rows), jnp.bfloat16),
        ],
        scratch_shapes=[pltpu.VMEM((HD, rows), jnp.float32), pltpu.VMEM((HD, rows), jnp.float32)],
        compiler_params=pltpu.CompilerParams(dimension_semantics=("arbitrary",)),
    )(queries, keys_values, keys_values, upstream, scales[:, None], segments[:, None], segments[None, :])


def front_kernel(dp_count, hidden_ref, query_ref, upstream_ref, hidden_later, query_later, upstream_later,
                 pick_ref, normed_ref, query_out, upstream_out, full, left_h, right_h, left_q, right_q,
                 left_u, right_u, right_sent, left_got, left_sent, right_got, mp_sent, mp_got):
    device, me = lax.axis_index("dp"), lax.axis_index("mp")
    half, core = me // 2, me % 2
    near, far, corner = half * 2 + 1 - core, (1 - half) * 2 + core, (1 - half) * 2 + 1 - core
    has_left, has_right = device > 0, device < dp_count - 1
    mesh_id = pl.DeviceIdType.MESH
    width = hidden_ref.shape[1]
    chunk = width // CHUNKS
    parts = []
    for array, later, from_left, from_right in (
        (hidden_ref, hidden_later, left_h, right_h),
        (query_ref, query_later, left_q, right_q),
        (upstream_ref, upstream_later, left_u, right_u),
    ):
        for at in range(0, array.shape[1], chunk):
            parts.append((array, later, from_left, from_right, slice(at, at + chunk)))

    def to_right(p):
        _, later, from_left, _, columns = parts[p]
        return pltpu.make_async_remote_copy(
            src_ref=later.at[:, columns], dst_ref=from_left.at[:, columns],
            send_sem=right_sent.at[p], recv_sem=left_got.at[p],
            device_id={"dp": device + 1}, device_id_type=mesh_id,
        )

    def to_left(p):
        array, _, _, from_right, columns = parts[p]
        return pltpu.make_async_remote_copy(
            src_ref=array.at[:PIECE, columns], dst_ref=from_right.at[:, columns],
            send_sem=left_sent.at[p], recv_sem=right_got.at[p],
            device_id={"dp": device - 1}, device_id_type=mesh_id,
        )

    def over_mp(kind, c):
        owner, target = ((me, near), (me, far), (far, near))[kind]
        columns = slice(c * chunk, (c + 1) * chunk)
        return pltpu.make_async_remote_copy(
            src_ref=full.at[owner, :, columns], dst_ref=full.at[owner, :, columns],
            send_sem=mp_sent.at[kind, c], recv_sem=mp_got.at[kind, c],
            device_id={"mp": target}, device_id_type=mesh_id,
        )

    def settled(p):
        array, _, from_left, from_right, columns = parts[p]

        @pl.when(has_left)
        def _():
            to_right(p).wait_recv()

        @pl.when(has_right)
        def _():
            to_left(p).wait_recv()

        own = PIECE + CAP_R
        total = jnp.dot(pick_ref[:, :PIECE], from_left[:, columns], preferred_element_type=jnp.float32)
        total += jnp.dot(pick_ref[:, PIECE:own], array[:, columns], preferred_element_type=jnp.float32)
        total += jnp.dot(pick_ref[:, own:], from_right[:, columns], preferred_element_type=jnp.float32)
        return total.astype(jnp.bfloat16)

    barrier = pltpu.get_barrier_semaphore()
    for target in (near, far):
        pl.semaphore_signal(barrier, inc=1, device_id={"mp": target}, device_id_type=mesh_id)

    @pl.when(has_left)
    def _():
        pl.semaphore_signal(barrier, inc=1, device_id={"dp": device - 1}, device_id_type=mesh_id)

    @pl.when(has_right)
    def _():
        pl.semaphore_signal(barrier, inc=1, device_id={"dp": device + 1}, device_id_type=mesh_id)

    @pl.when(has_left & has_right)
    def _():
        pl.semaphore_wait(barrier, 4)

    @pl.when(jnp.logical_not(has_left & has_right))
    def _():
        pl.semaphore_wait(barrier, 3)

    @pl.when(has_right)
    def _():
        for p in range(len(parts)):
            to_right(p).start()

    @pl.when(has_left)
    def _():
        for p in range(len(parts)):
            to_left(p).start()

    @pl.when(jnp.logical_not(has_left))
    def _():
        for ref in (left_h, left_q, left_u):
            ref[...] = jnp.zeros_like(ref)

    @pl.when(jnp.logical_not(has_right))
    def _():
        for ref in (right_h, right_q, right_u):
            ref[...] = jnp.zeros_like(ref)

    for c in range(CHUNKS):
        full[me, :, c * chunk : (c + 1) * chunk] = settled(c)
        over_mp(1, c).start()
        over_mp(0, c).start()
        if c > 0:
            over_mp(1, c - 1).wait_recv()
            over_mp(2, c - 1).start()
    for p in range(CHUNKS, len(parts)):
        target = query_out if parts[p][0] is query_ref else upstream_out
        target[:, parts[p][4]] = settled(p)
        if p == CHUNKS:
            over_mp(1, CHUNKS - 1).wait_recv()
            over_mp(2, CHUNKS - 1).start()
    for c in range(CHUNKS):
        over_mp(0, c).wait_recv()
        over_mp(2, c).wait_recv()

    owners, rows, _ = full.shape
    tile = 256
    squares = jnp.zeros((rows, HD), jnp.float32)
    for owner in range(owners):
        for at in range(0, width, HD):
            wide = full[owner, :, at : at + HD].astype(jnp.float32)
            squares += wide * wide
    scale = lax.rsqrt(jnp.sum(squares, axis=1, keepdims=True) / (owners * width) + epsilon)
    for owner in range(owners):
        for at in range(0, width, tile):
            wide = full[owner, :, at : at + tile].astype(jnp.float32)
            spot = owner * width + at
            normed_ref[:, spot : spot + tile] = (wide * scale).astype(jnp.bfloat16)

    @pl.when(has_right)
    def _():
        for p in range(len(parts)):
            to_right(p).wait_send()

    @pl.when(has_left)
    def _():
        for p in range(len(parts)):
            to_left(p).wait_send()

    for kind in range(3):
        for c in range(CHUNKS):
            over_mp(kind, c).wait_send()


def front(hidden, queries, upstream, own_piece, pick):
    width, head_width = hidden.shape[1], queries.shape[1]
    owners = lax.axis_size("mp")
    laters = [
        lax.dynamic_slice_in_dim(array, own_piece, PIECE, 0) for array in (hidden, queries, upstream)
    ]
    part_count = CHUNKS + 2 * (head_width * CHUNKS // width)
    vmem = pl.BlockSpec(memory_space=pltpu.VMEM)
    piece = lambda columns: pltpu.VMEM((PIECE, columns), jnp.bfloat16)
    part_sems = pltpu.SemaphoreType.DMA((part_count,))
    mp_sems = pltpu.SemaphoreType.DMA((3, CHUNKS))
    return pl.pallas_call(
        functools.partial(front_kernel, lax.axis_size("dp")),
        in_specs=[vmem] * 7,
        out_specs=[vmem] * 3,
        out_shape=[
            jax.ShapeDtypeStruct((CAP_L, owners * width), jnp.bfloat16),
            jax.ShapeDtypeStruct((CAP_L, head_width), jnp.bfloat16),
            jax.ShapeDtypeStruct((CAP_L, head_width), jnp.bfloat16),
        ],
        scratch_shapes=[
            pltpu.VMEM((owners, CAP_L, width), jnp.bfloat16),
            piece(width), piece(width),
            piece(head_width), piece(head_width),
            piece(head_width), piece(head_width),
            part_sems, part_sems, part_sems, part_sems, mp_sems, mp_sems,
        ],
        compiler_params=pltpu.CompilerParams(
            collective_id=1, has_side_effects=True, vmem_limit_bytes=40 * 1024 * 1024
        ),
    )(hidden, queries, upstream, *laters, pick)


def gradient_kernel(count, normed_ref, cots_ref, key_ref, value_ref, pair_out, pair_in, line_out,
                    line_in, acc, pair_sent, pair_got, line_sent, line_got):
    me = lax.axis_index("dp")
    lines = count // 2
    line, side = me // 2, me % 2
    width = acc.shape[1]
    mesh_id = pl.DeviceIdType.MESH

    def place(k):
        return (line + 1 + k) % lines

    def share(owner):
        columns = pl.ds(pl.multiple_of(owner * width, width), width)
        return jnp.dot(cots_ref[...], normed_ref[:, columns], preferred_element_type=jnp.float32)

    def pair_copy(k):
        return pltpu.make_async_remote_copy(
            src_ref=pair_out.at[k], dst_ref=pair_in.at[k],
            send_sem=pair_sent.at[k], recv_sem=pair_got.at[k],
            device_id={"dp": line * 2 + 1 - side}, device_id_type=mesh_id,
        )

    def line_copy(k):
        return pltpu.make_async_remote_copy(
            src_ref=line_out.at[k], dst_ref=line_in.at[k],
            send_sem=line_sent.at[k], recv_sem=line_got.at[k],
            device_id={"dp": place(k) * 2 + side}, device_id_type=mesh_id,
        )

    barrier = pltpu.get_barrier_semaphore()
    pl.semaphore_signal(barrier, inc=1, device_id={"dp": line * 2 + 1 - side}, device_id_type=mesh_id)

    @pl.loop(0, lines - 1)
    def _(k):
        pl.semaphore_signal(barrier, inc=1, device_id={"dp": place(k) * 2 + side}, device_id_type=mesh_id)

    pl.semaphore_wait(barrier, lines)

    @pl.loop(0, lines)
    def _(k):
        pair_out[k] = share(place(k) * 2 + 1 - side).astype(jnp.bfloat16)
        pair_copy(k).start()

    @pl.loop(0, lines - 1)
    def _(k):
        own = share(place(k) * 2 + side)
        pair_copy(k).wait_recv()
        line_out[k] = (own + pair_in[k].astype(jnp.float32)).astype(jnp.bfloat16)
        line_copy(k).start()

    acc[...] = share(me)
    pair_copy(lines - 1).wait_recv()
    acc[...] += pair_in[lines - 1].astype(jnp.float32)

    @pl.loop(0, lines - 1)
    def _(k):
        line_copy(k).wait_recv()
        acc[...] += line_in[k].astype(jnp.float32)

    key_ref[...] = acc[:HD].T
    value_ref[...] = acc[HD:].T

    @pl.loop(0, lines)
    def _(k):
        pair_copy(k).wait_send()

    @pl.loop(0, lines - 1)
    def _(k):
        line_copy(k).wait_send()


def gradient_sum(normed, cots):
    count = lax.axis_size("dp")
    lines = count // 2
    width = normed.shape[1] // count
    vmem = pl.BlockSpec(memory_space=pltpu.VMEM)
    shares = lambda n: pltpu.VMEM((n, 2 * HD, width), jnp.bfloat16)
    return pl.pallas_call(
        functools.partial(gradient_kernel, count),
        in_specs=[vmem, vmem],
        out_specs=[vmem, vmem],
        out_shape=[jax.ShapeDtypeStruct((width, HD), jnp.float32)] * 2,
        scratch_shapes=[
            shares(lines),
            shares(lines),
            shares(lines - 1),
            shares(lines - 1),
            pltpu.VMEM((2 * HD, width), jnp.float32),
            pltpu.SemaphoreType.DMA((lines,)),
            pltpu.SemaphoreType.DMA((lines,)),
            pltpu.SemaphoreType.DMA((lines - 1,)),
            pltpu.SemaphoreType.DMA((lines - 1,)),
        ],
        compiler_params=pltpu.CompilerParams(
            collective_id=0, has_side_effects=True, vmem_limit_bytes=40 * 1024 * 1024
        ),
    )(normed, cots)


def body(hidden, queries, upstream, key_weight, value_weight, lengths, advantage):
    device = lax.axis_index("dp")
    segments, scales, source, own_piece = learner_rows(lengths, advantage, device)
    positions = jnp.arange(2 * PIECE + CAP_R, dtype=jnp.int32)
    pick = (source[:, None] == positions[None, :]).astype(jnp.bfloat16)

    normed, query_rows, upstream_rows = front(hidden, queries, upstream, own_piece, pick)
    weight = jnp.concatenate([key_weight, value_weight], axis=1)
    keys_values = jnp.dot(normed, weight, preferred_element_type=jnp.float32).astype(jnp.bfloat16)
    attention_out, cots = attend(query_rows, keys_values, upstream_rows, scales, segments)
    key_grad, value_grad = gradient_sum(normed, cots)
    return (attention_out, key_grad, value_grad)


def solution(mesh):
    in_specs = (P("dp", "mp"), P("dp", "mp"), P("dp", "mp"), P(None, "mp"), P(None, "mp"), P(), P())
    out_specs = (P("dp", "mp"), P("dp", "mp"), P("dp", "mp"))
    return jax.shard_map(body, mesh=mesh, in_specs=in_specs, out_specs=out_specs, check_vma=False)
```

```python
import functools

import jax
import jax.numpy as jnp
from jax import lax
from jax.experimental import pallas as pl
from jax.experimental.pallas import tpu as pltpu
from jax.sharding import PartitionSpec as P

HD = 128
CAP_R = 512
CAP_L = 256
PIECE = 128
LAST_START = CAP_R - PIECE
CHUNKS = 4
AHEAD = 3

epsilon = 1e-06
masked_score = -1e30


def derive_moves(lengths):
    device_total, slot_total = lengths.shape
    used_slots = jnp.sum((lengths > 0).astype(jnp.int32), axis=1)
    heavy_flag = used_slots >= 6
    devices = jnp.arange(device_total, dtype=jnp.int32)
    left_heavy = jnp.concatenate([jnp.zeros((1,), bool), heavy_flag[:-1]])
    light_left = ((devices > 0) & jnp.logical_not(left_heavy)).astype(jnp.int32)
    sent_left = jnp.where(heavy_flag, (used_slots - 4) // 2, light_left)
    kept_count = jnp.where(heavy_flag, 4, 1).astype(jnp.int32)
    slot_ids = jnp.arange(slot_total, dtype=jnp.int32)[None, :]
    return jnp.where(
        slot_ids < sent_left[:, None],
        -1,
        jnp.where(
            slot_ids < (sent_left + kept_count)[:, None],
            0,
            jnp.where(slot_ids < used_slots[:, None], 1, 0),
        ),
    )


def learner_rows(lengths, advantage, device):
    device_total, slot_total = lengths.shape
    moves = derive_moves(lengths)
    slot_ids = jnp.arange(slot_total, dtype=jnp.int32)
    before = (slot_ids[:, None] < slot_ids[None, :]).astype(jnp.int32)
    begins = jnp.sum(lengths[:, :, None] * before[None], axis=1)
    piece_start = jnp.minimum(jnp.sum(jnp.where(moves < 1, lengths, 0), axis=1), LAST_START)
    bases = jnp.stack(
        [begins - piece_start[:, None], begins + PIECE, begins + PIECE + CAP_R], axis=0
    )
    table = jnp.pad(lengths, ((1, 1), (0, 0)))
    window = lax.dynamic_slice_in_dim(table, device, 3, 0)
    move_window = lax.dynamic_slice_in_dim(jnp.pad(moves, ((1, 1), (0, 0))), device, 3, 0)
    rate_window = lax.dynamic_slice_in_dim(jnp.pad(advantage, ((1, 1), (0, 0))), device, 3, 0)
    base_window = lax.dynamic_slice_in_dim(jnp.pad(bases, ((0, 0), (1, 1), (0, 0))), device, 3, 1)
    base_window = jnp.stack([base_window[0, 0], base_window[1, 1], base_window[2, 2]], axis=0)
    wanted = jnp.array([1, 0, -1], jnp.int32)[:, None]
    sizes = jnp.where(move_window == wanted, window, 0).reshape(-1)
    rates = rate_window.reshape(-1) / jnp.maximum(sizes, 1).astype(jnp.float32)
    places = base_window.reshape(-1)
    ids = jnp.arange(3 * slot_total, dtype=jnp.int32)
    starts = jnp.sum(jnp.where(ids[:, None] < ids[None, :], sizes[:, None], 0), axis=0)
    ends = starts + sizes
    rows = jnp.arange(CAP_L, dtype=jnp.int32)
    hits = (rows[:, None] >= starts[None, :]) & (rows[:, None] < ends[None, :])
    segments = jnp.sum((rows[:, None] >= ends[None, :]).astype(jnp.int32), axis=1)
    scales = jnp.sum(jnp.where(hits, rates[None, :], 0.0), axis=1)
    source = jnp.sum(jnp.where(hits, (places - starts)[None, :] + rows[:, None] + 1, 0), axis=1) - 1
    own_piece = lax.dynamic_index_in_dim(piece_start, device, 0, keepdims=False)
    return segments, scales, source, own_piece


def attention_kernel(q_ref, k_ref, v_ref, u_ref, scale_ref, seg_col_ref, seg_row_ref,
                     out_ref, cots_ref, key_acc, value_acc):
    head = pl.program_id(0)
    inverse_root = HD ** (-0.5)
    rows = q_ref.shape[0]
    query, key, value = q_ref[...], k_ref[...], v_ref[...]
    cot = (scale_ref[...] * u_ref[...].astype(jnp.float32)).astype(jnp.bfloat16)
    t = lax.broadcasted_iota(jnp.int32, (rows, rows), 0)
    u = lax.broadcasted_iota(jnp.int32, (rows, rows), 1)
    allowed = (u <= t) & (seg_col_ref[...] == seg_row_ref[...])
    across = (((1,), (1,)), ((), ()))
    down = (((0,), (0,)), ((), ()))
    scores = lax.dot_general(query, key, across, preferred_element_type=jnp.float32) * inverse_root
    scores = jnp.where(allowed, scores, masked_score)
    raised = jnp.exp(scores - jnp.max(scores, axis=-1, keepdims=True))
    probability = raised * (1.0 / jnp.sum(raised, axis=-1, keepdims=True))
    weights = probability.astype(jnp.bfloat16)
    out_ref[...] = jnp.dot(weights, value, preferred_element_type=jnp.float32).astype(jnp.bfloat16)
    prob_grad = lax.dot_general(cot, value, across, preferred_element_type=jnp.float32)
    centre = jnp.sum(probability * prob_grad, axis=-1, keepdims=True)
    score_grad = (probability * (prob_grad - centre)).astype(jnp.bfloat16)
    key_term = lax.dot_general(query, score_grad, down, preferred_element_type=jnp.float32)
    value_term = lax.dot_general(cot, weights, down, preferred_element_type=jnp.float32)

    @pl.when(head == 0)
    def _():
        key_acc[...] = key_term
        value_acc[...] = value_term

    @pl.when(head > 0)
    def _():
        key_acc[...] += key_term
        value_acc[...] += value_term

    @pl.when(head == pl.num_programs(0) - 1)
    def _():
        cots_ref[:HD] = (key_acc[...] * inverse_root).astype(jnp.bfloat16)
        cots_ref[HD:] = value_acc[...].astype(jnp.bfloat16)


def attend(queries, keys_values, upstream, scales, segments):
    rows, width = queries.shape
    head_block = pl.BlockSpec((rows, HD), lambda h: (0, h))
    whole = lambda shape: pl.BlockSpec(shape, lambda h: (0, 0))
    return pl.pallas_call(
        attention_kernel,
        grid=(width // HD,),
        in_specs=[
            head_block,
            pl.BlockSpec((rows, HD), lambda h: (0, 0)),
            pl.BlockSpec((rows, HD), lambda h: (0, 1)),
            head_block,
            whole((rows, 1)),
            whole((rows, 1)),
            whole((1, rows)),
        ],
        out_specs=[head_block, whole((2 * HD, rows))],
        out_shape=[
            jax.ShapeDtypeStruct((rows, width), jnp.bfloat16),
            jax.ShapeDtypeStruct((2 * HD, rows), jnp.bfloat16),
        ],
        scratch_shapes=[pltpu.VMEM((HD, rows), jnp.float32), pltpu.VMEM((HD, rows), jnp.float32)],
        compiler_params=pltpu.CompilerParams(dimension_semantics=("arbitrary",)),
    )(queries, keys_values, keys_values, upstream, scales[:, None], segments[:, None], segments[None, :])


def front_kernel(dp_count, hidden_hbm, query_hbm, upstream_hbm, key_hbm, value_hbm, hidden_later, query_later,
                 upstream_later, pick_ref, normed_ref, kv_ref, query_out, upstream_out, hidden_ref, query_ref,
                 upstream_ref, weight_ref, local_done, full, left_h, right_h, left_q, right_q,
                 left_u, right_u, right_sent, left_got, left_sent, right_got, mp_sent, mp_got):
    device, me = lax.axis_index("dp"), lax.axis_index("mp")
    half, core = me // 2, me % 2
    near, far, corner = half * 2 + 1 - core, (1 - half) * 2 + core, (1 - half) * 2 + 1 - core
    has_left, has_right = device > 0, device < dp_count - 1
    mesh_id = pl.DeviceIdType.MESH
    width = hidden_ref.shape[1]
    chunk = width // CHUNKS
    parts = []
    for array, source, later, from_left, from_right in (
        (hidden_ref, hidden_hbm, hidden_later, left_h, right_h),
        (query_ref, query_hbm, query_later, left_q, right_q),
        (upstream_ref, upstream_hbm, upstream_later, left_u, right_u),
    ):
        for at in range(0, array.shape[1], chunk):
            parts.append((array, later, from_left, from_right, slice(at, at + chunk), source))
    fetches = [
        pltpu.make_async_copy(source, target, local_done.at[n])
        for n, (source, target) in enumerate((
            (hidden_hbm, hidden_ref),
            (query_hbm, query_ref),
            (upstream_hbm, upstream_ref),
            (key_hbm, weight_ref.at[:, :HD]),
            (value_hbm, weight_ref.at[:, HD:]),
        ))
    ]

    def to_right(p):
        _, later, from_left, _, columns, _ = parts[p]
        return pltpu.make_async_remote_copy(
            src_ref=later.at[:, columns], dst_ref=from_left.at[:, columns],
            send_sem=right_sent.at[p], recv_sem=left_got.at[p],
            device_id={"dp": device + 1}, device_id_type=mesh_id,
        )

    def to_left(p):
        _, _, _, from_right, columns, source = parts[p]
        return pltpu.make_async_remote_copy(
            src_ref=source.at[:PIECE, columns], dst_ref=from_right.at[:, columns],
            send_sem=left_sent.at[p], recv_sem=right_got.at[p],
            device_id={"dp": device - 1}, device_id_type=mesh_id,
        )

    def over_mp(kind, c):
        owner, target = ((me, near), (me, far), (far, near))[kind]
        columns = slice(c * chunk, (c + 1) * chunk)
        return pltpu.make_async_remote_copy(
            src_ref=full.at[owner, :, columns], dst_ref=full.at[owner, :, columns],
            send_sem=mp_sent.at[kind, c], recv_sem=mp_got.at[kind, c],
            device_id={"mp": target}, device_id_type=mesh_id,
        )

    def settled(p):
        array, _, from_left, from_right, columns, _ = parts[p]

        @pl.when(has_left)
        def _():
            to_right(p).wait_recv()

        @pl.when(has_right)
        def _():
            to_left(p).wait_recv()

        own = PIECE + CAP_R
        total = jnp.dot(pick_ref[:, :PIECE], from_left[:, columns], preferred_element_type=jnp.float32)
        total += jnp.dot(pick_ref[:, PIECE:own], array[:, columns], preferred_element_type=jnp.float32)
        total += jnp.dot(pick_ref[:, own:], from_right[:, columns], preferred_element_type=jnp.float32)
        return total.astype(jnp.bfloat16)

    for fetch in fetches:
        fetch.start()
    barrier = pltpu.get_barrier_semaphore()
    for target in (near, far):
        pl.semaphore_signal(barrier, inc=1, device_id={"mp": target}, device_id_type=mesh_id)

    @pl.when(has_left)
    def _():
        pl.semaphore_signal(barrier, inc=1, device_id={"dp": device - 1}, device_id_type=mesh_id)

    @pl.when(has_right)
    def _():
        pl.semaphore_signal(barrier, inc=1, device_id={"dp": device + 1}, device_id_type=mesh_id)

    @pl.when(has_left & has_right)
    def _():
        pl.semaphore_wait(barrier, 4)

    @pl.when(jnp.logical_not(has_left & has_right))
    def _():
        pl.semaphore_wait(barrier, 3)

    @pl.when(has_right)
    def _():
        for p in range(len(parts)):
            to_right(p).start()

    @pl.when(has_left)
    def _():
        for p in range(len(parts)):
            to_left(p).start()

    @pl.when(jnp.logical_not(has_left))
    def _():
        for ref in (left_h, left_q, left_u):
            ref[...] = jnp.zeros_like(ref)

    @pl.when(jnp.logical_not(has_right))
    def _():
        for ref in (right_h, right_q, right_u):
            ref[...] = jnp.zeros_like(ref)

    fetches[0].wait()
    for c in range(CHUNKS):
        full[me, :, c * chunk : (c + 1) * chunk] = settled(c)
        over_mp(1, c).start()
        over_mp(0, c).start()
        if c > 0:
            over_mp(1, c - 1).wait_recv()
            over_mp(2, c - 1).start()
    over_mp(1, CHUNKS - 1).wait_recv()
    over_mp(2, CHUNKS - 1).start()
    for c in range(CHUNKS):
        over_mp(0, c).wait_recv()
        over_mp(2, c).wait_recv()

    owners, rows, _ = full.shape
    tile = 256
    squares = jnp.zeros((rows, HD), jnp.float32)
    for owner in range(owners):
        for at in range(0, width, HD):
            wide = full[owner, :, at : at + HD].astype(jnp.float32)
            squares += wide * wide
    scale = lax.rsqrt(jnp.sum(squares, axis=1, keepdims=True) / (owners * width) + epsilon)
    for owner in range(owners):
        for at in range(0, width, tile):
            wide = full[owner, :, at : at + tile].astype(jnp.float32)
            spot = owner * width + at
            normed_ref[:, spot : spot + tile] = (wide * scale).astype(jnp.bfloat16)
    fetches[3].wait()
    fetches[4].wait()
    kv_ref[...] = jnp.dot(
        normed_ref[...], weight_ref[...], preferred_element_type=jnp.float32
    ).astype(jnp.bfloat16)
    fetches[1].wait()
    fetches[2].wait()
    for p in range(CHUNKS, len(parts)):
        target = query_out if parts[p][0] is query_ref else upstream_out
        target[:, parts[p][4]] = settled(p)

    @pl.when(has_right)
    def _():
        for p in range(len(parts)):
            to_right(p).wait_send()

    @pl.when(has_left)
    def _():
        for p in range(len(parts)):
            to_left(p).wait_send()

    for kind in range(3):
        for c in range(CHUNKS):
            over_mp(kind, c).wait_send()


def front(hidden, queries, upstream, key_weight, value_weight, own_piece, pick):
    width, head_width = hidden.shape[1], queries.shape[1]
    owners = lax.axis_size("mp")
    laters = [
        lax.dynamic_slice_in_dim(array, own_piece, PIECE, 0) for array in (hidden, queries, upstream)
    ]
    part_count = CHUNKS + 2 * (head_width * CHUNKS // width)
    vmem = pl.BlockSpec(memory_space=pltpu.VMEM)
    piece = lambda columns: pltpu.VMEM((PIECE, columns), jnp.bfloat16)
    part_sems = pltpu.SemaphoreType.DMA((part_count,))
    mp_sems = pltpu.SemaphoreType.DMA((3, CHUNKS))
    return pl.pallas_call(
        functools.partial(front_kernel, lax.axis_size("dp")),
        in_specs=[pl.BlockSpec(memory_space=pl.ANY)] * 5 + [vmem] * 4,
        out_specs=[vmem] * 4,
        out_shape=[
            jax.ShapeDtypeStruct((CAP_L, owners * width), jnp.bfloat16),
            jax.ShapeDtypeStruct((CAP_L, 2 * HD), jnp.bfloat16),
            jax.ShapeDtypeStruct((CAP_L, head_width), jnp.bfloat16),
            jax.ShapeDtypeStruct((CAP_L, head_width), jnp.bfloat16),
        ],
        scratch_shapes=[
            pltpu.VMEM(hidden.shape, jnp.bfloat16),
            pltpu.VMEM(queries.shape, jnp.bfloat16),
            pltpu.VMEM(upstream.shape, jnp.bfloat16),
            pltpu.VMEM((owners * width, 2 * HD), jnp.bfloat16),
            pltpu.SemaphoreType.DMA((5,)),
            pltpu.VMEM((owners, CAP_L, width), jnp.bfloat16),
            piece(width), piece(width),
            piece(head_width), piece(head_width),
            piece(head_width), piece(head_width),
            part_sems, part_sems, part_sems, part_sems, mp_sems, mp_sems,
        ],
        compiler_params=pltpu.CompilerParams(
            collective_id=1, has_side_effects=True, vmem_limit_bytes=48 * 1024 * 1024
        ),
    )(hidden, queries, upstream, key_weight, value_weight, *laters, pick)


def gradient_kernel(count, normed_ref, cots_ref, key_ref, value_ref, pair_out, pair_in, line_out,
                    line_in, acc, pair_sent, pair_got, line_sent, line_got):
    me = lax.axis_index("dp")
    lines = count // 2
    line, side = me // 2, me % 2
    width = acc.shape[2]
    mesh_id = pl.DeviceIdType.MESH

    def place(k):
        return (line + 1 + k) % lines

    def share(p, of_side):
        owner = place(p // 2) * 2 + of_side
        columns = pl.ds(pl.multiple_of(owner * width, width), width)
        rows = pl.ds(pl.multiple_of(p % 2 * HD, HD), HD)
        return jnp.dot(cots_ref[rows], normed_ref[:, columns], preferred_element_type=jnp.float32)

    def pair_copy(k):
        return pltpu.make_async_remote_copy(
            src_ref=pair_out.at[k], dst_ref=pair_in.at[k],
            send_sem=pair_sent.at[k], recv_sem=pair_got.at[k],
            device_id={"dp": line * 2 + 1 - side}, device_id_type=mesh_id,
        )

    def line_copy(k):
        return pltpu.make_async_remote_copy(
            src_ref=line_out.at[k], dst_ref=line_in.at[k],
            send_sem=line_sent.at[k], recv_sem=line_got.at[k],
            device_id={"dp": place(k // 2) * 2 + side}, device_id_type=mesh_id,
        )

    barrier = pltpu.get_barrier_semaphore()
    pl.semaphore_signal(barrier, inc=1, device_id={"dp": line * 2 + 1 - side}, device_id_type=mesh_id)

    @pl.loop(0, lines - 1)
    def _(k):
        pl.semaphore_signal(barrier, inc=1, device_id={"dp": place(k) * 2 + side}, device_id_type=mesh_id)

    pl.semaphore_wait(barrier, lines)
    total = 2 * lines

    for p in range(AHEAD):
        pair_out[p] = share(p, 1 - side).astype(jnp.bfloat16)
        pair_copy(p).start()

    @pl.loop(0, total - 2)
    def _(p):
        own = share(p, side)

        @pl.when(p + AHEAD < total)
        def _():
            pair_out[p + AHEAD] = share(p + AHEAD, 1 - side).astype(jnp.bfloat16)

        pair_copy(p).wait_recv()

        @pl.when(p + AHEAD < total)
        def _():
            pair_copy(p + AHEAD).start()

        line_out[p] = (own + pair_in[p].astype(jnp.float32)).astype(jnp.bfloat16)
        line_copy(p).start()

    for h in range(2):
        acc[h] = share(total - 2 + h, side)
    for h in range(2):
        pair_copy(total - 2 + h).wait_recv()
        acc[h] += pair_in[total - 2 + h].astype(jnp.float32)

    @pl.loop(0, lines - 1)
    def _(k):
        for h in range(2):
            line_copy(2 * k + h).wait_recv()
            acc[h] += line_in[2 * k + h].astype(jnp.float32)

    key_ref[...] = acc[0].T
    value_ref[...] = acc[1].T

    @pl.loop(0, total)
    def _(p):
        pair_copy(p).wait_send()

    @pl.loop(0, total - 2)
    def _(p):
        line_copy(p).wait_send()


def gradient_sum(normed, cots):
    count = lax.axis_size("dp")
    lines = count // 2
    width = normed.shape[1] // count
    vmem = pl.BlockSpec(memory_space=pltpu.VMEM)
    shares = lambda n: pltpu.VMEM((2 * n, HD, width), jnp.bfloat16)
    return pl.pallas_call(
        functools.partial(gradient_kernel, count),
        in_specs=[vmem, vmem],
        out_specs=[vmem, vmem],
        out_shape=[jax.ShapeDtypeStruct((width, HD), jnp.float32)] * 2,
        scratch_shapes=[
            shares(lines),
            shares(lines),
            shares(lines - 1),
            shares(lines - 1),
            pltpu.VMEM((2, HD, width), jnp.float32),
            pltpu.SemaphoreType.DMA((2 * lines,)),
            pltpu.SemaphoreType.DMA((2 * lines,)),
            pltpu.SemaphoreType.DMA((2 * lines - 2,)),
            pltpu.SemaphoreType.DMA((2 * lines - 2,)),
        ],
        compiler_params=pltpu.CompilerParams(
            collective_id=0, has_side_effects=True, vmem_limit_bytes=40 * 1024 * 1024
        ),
    )(normed, cots)


def body(hidden, queries, upstream, key_weight, value_weight, lengths, advantage):
    device = lax.axis_index("dp")
    segments, scales, source, own_piece = learner_rows(lengths, advantage, device)
    positions = jnp.arange(2 * PIECE + CAP_R, dtype=jnp.int32)
    pick = (source[:, None] == positions[None, :]).astype(jnp.bfloat16)

    normed, keys_values, query_rows, upstream_rows = front(
        hidden, queries, upstream, key_weight, value_weight, own_piece, pick
    )
    attention_out, cots = attend(query_rows, keys_values, upstream_rows, scales, segments)
    key_grad, value_grad = gradient_sum(normed, cots)
    return (attention_out, key_grad, value_grad)


def solution(mesh):
    in_specs = (P("dp", "mp"), P("dp", "mp"), P("dp", "mp"), P(None, "mp"), P(None, "mp"), P(), P())
    out_specs = (P("dp", "mp"), P("dp", "mp"), P("dp", "mp"))
    return jax.shard_map(body, mesh=mesh, in_specs=in_specs, out_specs=out_specs, check_vma=False)
```

```python
import functools

import jax
import jax.numpy as jnp
from jax import lax
from jax.experimental import pallas as pl
from jax.experimental.pallas import tpu as pltpu
from jax.sharding import PartitionSpec as P

HD = 128
CAP_R = 512
CAP_L = 256
PIECE = 128
LAST_START = CAP_R - PIECE
CHUNKS = 4
AHEAD = 3

epsilon = 1e-06
masked_score = -1e30


def derive_moves(lengths):
    device_total, slot_total = lengths.shape
    used_slots = jnp.sum((lengths > 0).astype(jnp.int32), axis=1)
    heavy_flag = used_slots >= 6
    devices = jnp.arange(device_total, dtype=jnp.int32)
    left_heavy = jnp.concatenate([jnp.zeros((1,), bool), heavy_flag[:-1]])
    light_left = ((devices > 0) & jnp.logical_not(left_heavy)).astype(jnp.int32)
    sent_left = jnp.where(heavy_flag, (used_slots - 4) // 2, light_left)
    kept_count = jnp.where(heavy_flag, 4, 1).astype(jnp.int32)
    slot_ids = jnp.arange(slot_total, dtype=jnp.int32)[None, :]
    return jnp.where(
        slot_ids < sent_left[:, None],
        -1,
        jnp.where(
            slot_ids < (sent_left + kept_count)[:, None],
            0,
            jnp.where(slot_ids < used_slots[:, None], 1, 0),
        ),
    )


def learner_rows(lengths, advantage, device):
    device_total, slot_total = lengths.shape
    moves = derive_moves(lengths)
    slot_ids = jnp.arange(slot_total, dtype=jnp.int32)
    before = (slot_ids[:, None] < slot_ids[None, :]).astype(jnp.int32)
    begins = jnp.sum(lengths[:, :, None] * before[None], axis=1)
    piece_start = jnp.minimum(jnp.sum(jnp.where(moves < 1, lengths, 0), axis=1), LAST_START)
    bases = jnp.stack(
        [begins - piece_start[:, None], begins + PIECE, begins + PIECE + CAP_R], axis=0
    )
    table = jnp.pad(lengths, ((1, 1), (0, 0)))
    window = lax.dynamic_slice_in_dim(table, device, 3, 0)
    move_window = lax.dynamic_slice_in_dim(jnp.pad(moves, ((1, 1), (0, 0))), device, 3, 0)
    rate_window = lax.dynamic_slice_in_dim(jnp.pad(advantage, ((1, 1), (0, 0))), device, 3, 0)
    base_window = lax.dynamic_slice_in_dim(jnp.pad(bases, ((0, 0), (1, 1), (0, 0))), device, 3, 1)
    base_window = jnp.stack([base_window[0, 0], base_window[1, 1], base_window[2, 2]], axis=0)
    wanted = jnp.array([1, 0, -1], jnp.int32)[:, None]
    sizes = jnp.where(move_window == wanted, window, 0).reshape(-1)
    rates = rate_window.reshape(-1) / jnp.maximum(sizes, 1).astype(jnp.float32)
    places = base_window.reshape(-1)
    ids = jnp.arange(3 * slot_total, dtype=jnp.int32)
    starts = jnp.sum(jnp.where(ids[:, None] < ids[None, :], sizes[:, None], 0), axis=0)
    ends = starts + sizes
    rows = jnp.arange(CAP_L, dtype=jnp.int32)
    hits = (rows[:, None] >= starts[None, :]) & (rows[:, None] < ends[None, :])
    segments = jnp.sum((rows[:, None] >= ends[None, :]).astype(jnp.int32), axis=1)
    scales = jnp.sum(jnp.where(hits, rates[None, :], 0.0), axis=1)
    source = jnp.sum(jnp.where(hits, (places - starts)[None, :] + rows[:, None] + 1, 0), axis=1) - 1
    own_piece = lax.dynamic_index_in_dim(piece_start, device, 0, keepdims=False)
    return segments, scales, source, own_piece


def attention_kernel(q_ref, k_ref, v_ref, u_ref, scale_ref, seg_col_ref, seg_row_ref,
                     out_ref, cots_ref, key_acc, value_acc):
    head = pl.program_id(0)
    inverse_root = HD ** (-0.5)
    rows = q_ref.shape[0]
    query, key, value = q_ref[...], k_ref[...], v_ref[...]
    cot = (scale_ref[...] * u_ref[...].astype(jnp.float32)).astype(jnp.bfloat16)
    t = lax.broadcasted_iota(jnp.int32, (rows, rows), 0)
    u = lax.broadcasted_iota(jnp.int32, (rows, rows), 1)
    allowed = (u <= t) & (seg_col_ref[...] == seg_row_ref[...])
    across = (((1,), (1,)), ((), ()))
    down = (((0,), (0,)), ((), ()))
    scores = lax.dot_general(query, key, across, preferred_element_type=jnp.float32) * inverse_root
    scores = jnp.where(allowed, scores, masked_score)
    raised = jnp.exp(scores - jnp.max(scores, axis=-1, keepdims=True))
    probability = raised * (1.0 / jnp.sum(raised, axis=-1, keepdims=True))
    weights = probability.astype(jnp.bfloat16)
    out_ref[...] = jnp.dot(weights, value, preferred_element_type=jnp.float32).astype(jnp.bfloat16)
    prob_grad = lax.dot_general(cot, value, across, preferred_element_type=jnp.float32)
    centre = jnp.sum(probability * prob_grad, axis=-1, keepdims=True)
    score_grad = (probability * (prob_grad - centre)).astype(jnp.bfloat16)
    key_term = lax.dot_general(query, score_grad, down, preferred_element_type=jnp.float32)
    value_term = lax.dot_general(cot, weights, down, preferred_element_type=jnp.float32)

    @pl.when(head == 0)
    def _():
        key_acc[...] = key_term
        value_acc[...] = value_term

    @pl.when(head > 0)
    def _():
        key_acc[...] += key_term
        value_acc[...] += value_term

    @pl.when(head == pl.num_programs(0) - 1)
    def _():
        cots_ref[:HD] = (key_acc[...] * inverse_root).astype(jnp.bfloat16)
        cots_ref[HD:] = value_acc[...].astype(jnp.bfloat16)


def attend(queries, keys_values, upstream, scales, segments):
    rows, width = queries.shape
    head_block = pl.BlockSpec((rows, HD), lambda h: (0, h))
    whole = lambda shape: pl.BlockSpec(shape, lambda h: (0, 0))
    return pl.pallas_call(
        attention_kernel,
        grid=(width // HD,),
        in_specs=[
            head_block,
            pl.BlockSpec((rows, HD), lambda h: (0, 0)),
            pl.BlockSpec((rows, HD), lambda h: (0, 1)),
            head_block,
            whole((rows, 1)),
            whole((rows, 1)),
            whole((1, rows)),
        ],
        out_specs=[head_block, whole((2 * HD, rows))],
        out_shape=[
            jax.ShapeDtypeStruct((rows, width), jnp.bfloat16),
            jax.ShapeDtypeStruct((2 * HD, rows), jnp.bfloat16),
        ],
        scratch_shapes=[pltpu.VMEM((HD, rows), jnp.float32), pltpu.VMEM((HD, rows), jnp.float32)],
        compiler_params=pltpu.CompilerParams(dimension_semantics=("arbitrary",)),
    )(queries, keys_values, keys_values, upstream, scales[:, None], segments[:, None], segments[None, :])


def front_kernel(dp_count, hidden_hbm, query_hbm, upstream_hbm, key_hbm, value_hbm, hidden_later, query_later,
                 upstream_later, pick_ref, normed_ref, kv_ref, query_out, upstream_out, hidden_ref, query_ref,
                 upstream_ref, weight_ref, local_done, full, left_h, right_h, left_q, right_q,
                 left_u, right_u, right_sent, left_got, left_sent, right_got, mp_sent, mp_got):
    device, me = lax.axis_index("dp"), lax.axis_index("mp")
    half, core = me // 2, me % 2
    near, far, corner = half * 2 + 1 - core, (1 - half) * 2 + core, (1 - half) * 2 + 1 - core
    has_left, has_right = device > 0, device < dp_count - 1
    mesh_id = pl.DeviceIdType.MESH
    width = hidden_ref.shape[1]
    chunk = width // CHUNKS
    parts = []
    for array, source, later, from_left, from_right in (
        (hidden_ref, hidden_hbm, hidden_later, left_h, right_h),
        (query_ref, query_hbm, query_later, left_q, right_q),
        (upstream_ref, upstream_hbm, upstream_later, left_u, right_u),
    ):
        for at in range(0, array.shape[1], chunk):
            parts.append((array, later, from_left, from_right, slice(at, at + chunk), source))
    fetches = [
        pltpu.make_async_copy(source, target, local_done.at[n])
        for n, (source, target) in enumerate((
            (hidden_hbm, hidden_ref),
            (query_hbm, query_ref),
            (upstream_hbm, upstream_ref),
            (key_hbm, weight_ref.at[:, :HD]),
            (value_hbm, weight_ref.at[:, HD:]),
        ))
    ]

    def to_right(p):
        _, later, from_left, _, columns, _ = parts[p]
        return pltpu.make_async_remote_copy(
            src_ref=later.at[:, columns], dst_ref=from_left.at[:, columns],
            send_sem=right_sent.at[p], recv_sem=left_got.at[p],
            device_id={"dp": device + 1}, device_id_type=mesh_id,
        )

    def to_left(p):
        _, _, _, from_right, columns, source = parts[p]
        return pltpu.make_async_remote_copy(
            src_ref=source.at[:PIECE, columns], dst_ref=from_right.at[:, columns],
            send_sem=left_sent.at[p], recv_sem=right_got.at[p],
            device_id={"dp": device - 1}, device_id_type=mesh_id,
        )

    def over_mp(kind, c):
        owner, target = ((me, near), (me, far), (far, near))[kind]
        columns = slice(c * chunk, (c + 1) * chunk)
        return pltpu.make_async_remote_copy(
            src_ref=full.at[owner, :, columns], dst_ref=full.at[owner, :, columns],
            send_sem=mp_sent.at[kind, c], recv_sem=mp_got.at[kind, c],
            device_id={"mp": target}, device_id_type=mesh_id,
        )

    def settled(p):
        array, _, from_left, from_right, columns, _ = parts[p]

        @pl.when(has_left)
        def _():
            to_right(p).wait_recv()

        @pl.when(has_right)
        def _():
            to_left(p).wait_recv()

        own = PIECE + CAP_R
        total = jnp.dot(pick_ref[:, :PIECE], from_left[:, columns], preferred_element_type=jnp.float32)
        total += jnp.dot(pick_ref[:, PIECE:own], array[:, columns], preferred_element_type=jnp.float32)
        total += jnp.dot(pick_ref[:, own:], from_right[:, columns], preferred_element_type=jnp.float32)
        return total.astype(jnp.bfloat16)

    for fetch in fetches:
        fetch.start()
    barrier = pltpu.get_barrier_semaphore()
    for target in (near, far):
        pl.semaphore_signal(barrier, inc=1, device_id={"mp": target}, device_id_type=mesh_id)

    @pl.when(has_left)
    def _():
        pl.semaphore_signal(barrier, inc=1, device_id={"dp": device - 1}, device_id_type=mesh_id)

    @pl.when(has_right)
    def _():
        pl.semaphore_signal(barrier, inc=1, device_id={"dp": device + 1}, device_id_type=mesh_id)

    @pl.when(has_left & has_right)
    def _():
        pl.semaphore_wait(barrier, 4)

    @pl.when(jnp.logical_not(has_left & has_right))
    def _():
        pl.semaphore_wait(barrier, 3)

    def send(these):
        @pl.when(has_right)
        def _():
            for p in these:
                to_right(p).start()

        @pl.when(has_left)
        def _():
            for p in these:
                to_left(p).start()

    send(range(CHUNKS))

    @pl.when(jnp.logical_not(has_left))
    def _():
        for ref in (left_h, left_q, left_u):
            ref[...] = jnp.zeros_like(ref)

    @pl.when(jnp.logical_not(has_right))
    def _():
        for ref in (right_h, right_q, right_u):
            ref[...] = jnp.zeros_like(ref)

    fetches[0].wait()
    for c in range(CHUNKS):
        full[me, :, c * chunk : (c + 1) * chunk] = settled(c)
        send(range(CHUNKS + c, len(parts), CHUNKS))
        over_mp(1, c).start()
        over_mp(0, c).start()
        if c > 0:
            over_mp(1, c - 1).wait_recv()
            over_mp(2, c - 1).start()
    over_mp(1, CHUNKS - 1).wait_recv()
    over_mp(2, CHUNKS - 1).start()
    for c in range(CHUNKS):
        over_mp(0, c).wait_recv()
        over_mp(2, c).wait_recv()

    owners, rows, _ = full.shape
    tile = 256
    squares = jnp.zeros((rows, HD), jnp.float32)
    for owner in range(owners):
        for at in range(0, width, HD):
            wide = full[owner, :, at : at + HD].astype(jnp.float32)
            squares += wide * wide
    scale = lax.rsqrt(jnp.sum(squares, axis=1, keepdims=True) / (owners * width) + epsilon)
    for owner in range(owners):
        for at in range(0, width, tile):
            wide = full[owner, :, at : at + tile].astype(jnp.float32)
            spot = owner * width + at
            normed_ref[:, spot : spot + tile] = (wide * scale).astype(jnp.bfloat16)
    fetches[3].wait()
    fetches[4].wait()
    kv_ref[...] = jnp.dot(
        normed_ref[...], weight_ref[...], preferred_element_type=jnp.float32
    ).astype(jnp.bfloat16)
    fetches[1].wait()
    fetches[2].wait()
    for p in range(CHUNKS, len(parts)):
        target = query_out if parts[p][0] is query_ref else upstream_out
        target[:, parts[p][4]] = settled(p)

    @pl.when(has_right)
    def _():
        for p in range(len(parts)):
            to_right(p).wait_send()

    @pl.when(has_left)
    def _():
        for p in range(len(parts)):
            to_left(p).wait_send()

    for kind in range(3):
        for c in range(CHUNKS):
            over_mp(kind, c).wait_send()


def front(hidden, queries, upstream, key_weight, value_weight, own_piece, pick):
    width, head_width = hidden.shape[1], queries.shape[1]
    owners = lax.axis_size("mp")
    laters = [
        lax.dynamic_slice_in_dim(array, own_piece, PIECE, 0) for array in (hidden, queries, upstream)
    ]
    part_count = CHUNKS + 2 * (head_width * CHUNKS // width)
    vmem = pl.BlockSpec(memory_space=pltpu.VMEM)
    piece = lambda columns: pltpu.VMEM((PIECE, columns), jnp.bfloat16)
    part_sems = pltpu.SemaphoreType.DMA((part_count,))
    mp_sems = pltpu.SemaphoreType.DMA((3, CHUNKS))
    return pl.pallas_call(
        functools.partial(front_kernel, lax.axis_size("dp")),
        in_specs=[pl.BlockSpec(memory_space=pl.ANY)] * 5 + [vmem] * 4,
        out_specs=[vmem] * 4,
        out_shape=[
            jax.ShapeDtypeStruct((CAP_L, owners * width), jnp.bfloat16),
            jax.ShapeDtypeStruct((CAP_L, 2 * HD), jnp.bfloat16),
            jax.ShapeDtypeStruct((CAP_L, head_width), jnp.bfloat16),
            jax.ShapeDtypeStruct((CAP_L, head_width), jnp.bfloat16),
        ],
        scratch_shapes=[
            pltpu.VMEM(hidden.shape, jnp.bfloat16),
            pltpu.VMEM(queries.shape, jnp.bfloat16),
            pltpu.VMEM(upstream.shape, jnp.bfloat16),
            pltpu.VMEM((owners * width, 2 * HD), jnp.bfloat16),
            pltpu.SemaphoreType.DMA((5,)),
            pltpu.VMEM((owners, CAP_L, width), jnp.bfloat16),
            piece(width), piece(width),
            piece(head_width), piece(head_width),
            piece(head_width), piece(head_width),
            part_sems, part_sems, part_sems, part_sems, mp_sems, mp_sems,
        ],
        compiler_params=pltpu.CompilerParams(
            collective_id=1, has_side_effects=True, vmem_limit_bytes=48 * 1024 * 1024
        ),
    )(hidden, queries, upstream, key_weight, value_weight, *laters, pick)


def gradient_kernel(count, normed_ref, cots_ref, key_ref, value_ref, pair_out, pair_in, line_out,
                    line_in, acc, pair_sent, pair_got, line_sent, line_got):
    me = lax.axis_index("dp")
    lines = count // 2
    line, side = me // 2, me % 2
    width = acc.shape[2]
    mesh_id = pl.DeviceIdType.MESH

    def place(k):
        return (line + 1 + k) % lines

    def share(p, of_side):
        owner = place(p // 2) * 2 + of_side
        columns = pl.ds(pl.multiple_of(owner * width, width), width)
        rows = pl.ds(pl.multiple_of(p % 2 * HD, HD), HD)
        return jnp.dot(cots_ref[rows], normed_ref[:, columns], preferred_element_type=jnp.float32)

    def pair_copy(k):
        return pltpu.make_async_remote_copy(
            src_ref=pair_out.at[k], dst_ref=pair_in.at[k],
            send_sem=pair_sent.at[k], recv_sem=pair_got.at[k],
            device_id={"dp": line * 2 + 1 - side}, device_id_type=mesh_id,
        )

    def line_copy(k):
        return pltpu.make_async_remote_copy(
            src_ref=line_out.at[k], dst_ref=line_in.at[k],
            send_sem=line_sent.at[k], recv_sem=line_got.at[k],
            device_id={"dp": place(k // 2) * 2 + side}, device_id_type=mesh_id,
        )

    barrier = pltpu.get_barrier_semaphore()
    pl.semaphore_signal(barrier, inc=1, device_id={"dp": line * 2 + 1 - side}, device_id_type=mesh_id)

    @pl.loop(0, lines - 1)
    def _(k):
        pl.semaphore_signal(barrier, inc=1, device_id={"dp": place(k) * 2 + side}, device_id_type=mesh_id)

    pl.semaphore_wait(barrier, lines)
    total = 2 * lines

    for p in range(AHEAD):
        pair_out[p] = share(p, 1 - side).astype(jnp.bfloat16)
        pair_copy(p).start()

    @pl.loop(0, total - 2)
    def _(p):
        own = share(p, side)

        @pl.when(p + AHEAD < total)
        def _():
            pair_out[p + AHEAD] = share(p + AHEAD, 1 - side).astype(jnp.bfloat16)

        pair_copy(p).wait_recv()

        @pl.when(p + AHEAD < total)
        def _():
            pair_copy(p + AHEAD).start()

        line_out[p] = (own + pair_in[p].astype(jnp.float32)).astype(jnp.bfloat16)
        line_copy(p).start()

    for h in range(2):
        acc[h] = share(total - 2 + h, side)
    for h in range(2):
        pair_copy(total - 2 + h).wait_recv()
        acc[h] += pair_in[total - 2 + h].astype(jnp.float32)

    @pl.loop(0, lines - 1)
    def _(k):
        for h in range(2):
            line_copy(2 * k + h).wait_recv()
            acc[h] += line_in[2 * k + h].astype(jnp.float32)

    key_ref[...] = acc[0].T
    value_ref[...] = acc[1].T

    @pl.loop(0, total)
    def _(p):
        pair_copy(p).wait_send()

    @pl.loop(0, total - 2)
    def _(p):
        line_copy(p).wait_send()


def gradient_sum(normed, cots):
    count = lax.axis_size("dp")
    lines = count // 2
    width = normed.shape[1] // count
    vmem = pl.BlockSpec(memory_space=pltpu.VMEM)
    shares = lambda n: pltpu.VMEM((2 * n, HD, width), jnp.bfloat16)
    return pl.pallas_call(
        functools.partial(gradient_kernel, count),
        in_specs=[vmem, vmem],
        out_specs=[vmem, vmem],
        out_shape=[jax.ShapeDtypeStruct((width, HD), jnp.float32)] * 2,
        scratch_shapes=[
            shares(lines),
            shares(lines),
            shares(lines - 1),
            shares(lines - 1),
            pltpu.VMEM((2, HD, width), jnp.float32),
            pltpu.SemaphoreType.DMA((2 * lines,)),
            pltpu.SemaphoreType.DMA((2 * lines,)),
            pltpu.SemaphoreType.DMA((2 * lines - 2,)),
            pltpu.SemaphoreType.DMA((2 * lines - 2,)),
        ],
        compiler_params=pltpu.CompilerParams(
            collective_id=0, has_side_effects=True, vmem_limit_bytes=40 * 1024 * 1024
        ),
    )(normed, cots)


def body(hidden, queries, upstream, key_weight, value_weight, lengths, advantage):
    device = lax.axis_index("dp")
    segments, scales, source, own_piece = learner_rows(lengths, advantage, device)
    positions = jnp.arange(2 * PIECE + CAP_R, dtype=jnp.int32)
    pick = (source[:, None] == positions[None, :]).astype(jnp.bfloat16)

    normed, keys_values, query_rows, upstream_rows = front(
        hidden, queries, upstream, key_weight, value_weight, own_piece, pick
    )
    attention_out, cots = attend(query_rows, keys_values, upstream_rows, scales, segments)
    key_grad, value_grad = gradient_sum(normed, cots)
    return (attention_out, key_grad, value_grad)


def solution(mesh):
    in_specs = (P("dp", "mp"), P("dp", "mp"), P("dp", "mp"), P(None, "mp"), P(None, "mp"), P(), P())
    out_specs = (P("dp", "mp"), P("dp", "mp"), P("dp", "mp"))
    return jax.shard_map(body, mesh=mesh, in_specs=in_specs, out_specs=out_specs, check_vma=False)
```

```python
import functools

import jax
import jax.numpy as jnp
from jax import lax
from jax.experimental import pallas as pl
from jax.experimental.pallas import tpu as pltpu
from jax.sharding import PartitionSpec as P

HD = 128
CAP_R = 512
CAP_L = 256
PIECE = 128
LAST_START = CAP_R - PIECE
CHUNKS = 4
AHEAD = 2

epsilon = 1e-06
masked_score = -1e30


def derive_moves(lengths):
    device_total, slot_total = lengths.shape
    used_slots = jnp.sum((lengths > 0).astype(jnp.int32), axis=1)
    heavy_flag = used_slots >= 6
    devices = jnp.arange(device_total, dtype=jnp.int32)
    left_heavy = jnp.concatenate([jnp.zeros((1,), bool), heavy_flag[:-1]])
    light_left = ((devices > 0) & jnp.logical_not(left_heavy)).astype(jnp.int32)
    sent_left = jnp.where(heavy_flag, (used_slots - 4) // 2, light_left)
    kept_count = jnp.where(heavy_flag, 4, 1).astype(jnp.int32)
    slot_ids = jnp.arange(slot_total, dtype=jnp.int32)[None, :]
    return jnp.where(
        slot_ids < sent_left[:, None],
        -1,
        jnp.where(
            slot_ids < (sent_left + kept_count)[:, None],
            0,
            jnp.where(slot_ids < used_slots[:, None], 1, 0),
        ),
    )


def learner_rows(lengths, advantage, device):
    device_total, slot_total = lengths.shape
    moves = derive_moves(lengths)
    slot_ids = jnp.arange(slot_total, dtype=jnp.int32)
    before = (slot_ids[:, None] < slot_ids[None, :]).astype(jnp.int32)
    begins = jnp.sum(lengths[:, :, None] * before[None], axis=1)
    piece_start = jnp.minimum(jnp.sum(jnp.where(moves < 1, lengths, 0), axis=1), LAST_START)
    bases = jnp.stack(
        [begins - piece_start[:, None], begins + PIECE, begins + PIECE + CAP_R], axis=0
    )
    table = jnp.pad(lengths, ((1, 1), (0, 0)))
    window = lax.dynamic_slice_in_dim(table, device, 3, 0)
    move_window = lax.dynamic_slice_in_dim(jnp.pad(moves, ((1, 1), (0, 0))), device, 3, 0)
    rate_window = lax.dynamic_slice_in_dim(jnp.pad(advantage, ((1, 1), (0, 0))), device, 3, 0)
    base_window = lax.dynamic_slice_in_dim(jnp.pad(bases, ((0, 0), (1, 1), (0, 0))), device, 3, 1)
    base_window = jnp.stack([base_window[0, 0], base_window[1, 1], base_window[2, 2]], axis=0)
    wanted = jnp.array([1, 0, -1], jnp.int32)[:, None]
    sizes = jnp.where(move_window == wanted, window, 0).reshape(-1)
    rates = rate_window.reshape(-1) / jnp.maximum(sizes, 1).astype(jnp.float32)
    places = base_window.reshape(-1)
    ids = jnp.arange(3 * slot_total, dtype=jnp.int32)
    starts = jnp.sum(jnp.where(ids[:, None] < ids[None, :], sizes[:, None], 0), axis=0)
    ends = starts + sizes
    rows = jnp.arange(CAP_L, dtype=jnp.int32)
    hits = (rows[:, None] >= starts[None, :]) & (rows[:, None] < ends[None, :])
    segments = jnp.sum((rows[:, None] >= ends[None, :]).astype(jnp.int32), axis=1)
    scales = jnp.sum(jnp.where(hits, rates[None, :], 0.0), axis=1)
    source = jnp.sum(jnp.where(hits, (places - starts)[None, :] + rows[:, None] + 1, 0), axis=1) - 1
    own_piece = lax.dynamic_index_in_dim(piece_start, device, 0, keepdims=False)
    return segments, scales, source, own_piece


def attention_kernel(q_ref, k_ref, v_ref, u_ref, scale_ref, seg_col_ref, seg_row_ref,
                     out_ref, cots_ref, key_acc, value_acc):
    head = pl.program_id(0)
    inverse_root = HD ** (-0.5)
    rows = q_ref.shape[0]
    query, key, value = q_ref[...], k_ref[...], v_ref[...]
    cot = (scale_ref[...] * u_ref[...].astype(jnp.float32)).astype(jnp.bfloat16)
    t = lax.broadcasted_iota(jnp.int32, (rows, rows), 0)
    u = lax.broadcasted_iota(jnp.int32, (rows, rows), 1)
    allowed = (u <= t) & (seg_col_ref[...] == seg_row_ref[...])
    across = (((1,), (1,)), ((), ()))
    down = (((0,), (0,)), ((), ()))
    scores = lax.dot_general(query, key, across, preferred_element_type=jnp.float32) * inverse_root
    scores = jnp.where(allowed, scores, masked_score)
    raised = jnp.exp(scores - jnp.max(scores, axis=-1, keepdims=True))
    probability = raised * (1.0 / jnp.sum(raised, axis=-1, keepdims=True))
    weights = probability.astype(jnp.bfloat16)
    out_ref[...] = jnp.dot(weights, value, preferred_element_type=jnp.float32).astype(jnp.bfloat16)
    prob_grad = lax.dot_general(cot, value, across, preferred_element_type=jnp.float32)
    centre = jnp.sum(probability * prob_grad, axis=-1, keepdims=True)
    score_grad = (probability * (prob_grad - centre)).astype(jnp.bfloat16)
    key_term = lax.dot_general(query, score_grad, down, preferred_element_type=jnp.float32)
    value_term = lax.dot_general(cot, weights, down, preferred_element_type=jnp.float32)

    @pl.when(head == 0)
    def _():
        key_acc[...] = key_term
        value_acc[...] = value_term

    @pl.when(head > 0)
    def _():
        key_acc[...] += key_term
        value_acc[...] += value_term

    @pl.when(head == pl.num_programs(0) - 1)
    def _():
        cots_ref[:HD] = (key_acc[...] * inverse_root).astype(jnp.bfloat16)
        cots_ref[HD:] = value_acc[...].astype(jnp.bfloat16)


def attend(queries, keys_values, upstream, scales, segments):
    rows, width = queries.shape
    head_block = pl.BlockSpec((rows, HD), lambda h: (0, h))
    whole = lambda shape: pl.BlockSpec(shape, lambda h: (0, 0))
    return pl.pallas_call(
        attention_kernel,
        grid=(width // HD,),
        in_specs=[
            head_block,
            pl.BlockSpec((rows, HD), lambda h: (0, 0)),
            pl.BlockSpec((rows, HD), lambda h: (0, 1)),
            head_block,
            whole((rows, 1)),
            whole((rows, 1)),
            whole((1, rows)),
        ],
        out_specs=[head_block, whole((2 * HD, rows))],
        out_shape=[
            jax.ShapeDtypeStruct((rows, width), jnp.bfloat16),
            jax.ShapeDtypeStruct((2 * HD, rows), jnp.bfloat16),
        ],
        scratch_shapes=[pltpu.VMEM((HD, rows), jnp.float32), pltpu.VMEM((HD, rows), jnp.float32)],
        compiler_params=pltpu.CompilerParams(dimension_semantics=("arbitrary",)),
    )(queries, keys_values, keys_values, upstream, scales[:, None], segments[:, None], segments[None, :])


def front_kernel(dp_count, hidden_hbm, query_hbm, upstream_hbm, key_hbm, value_hbm, hidden_later, query_later,
                 upstream_later, pick_ref, normed_ref, kv_ref, query_out, upstream_out, hidden_ref, query_ref,
                 upstream_ref, weight_ref, local_done, full, left_h, right_h, left_q, right_q,
                 left_u, right_u, right_sent, left_got, left_sent, right_got, mp_sent, mp_got):
    device, me = lax.axis_index("dp"), lax.axis_index("mp")
    half, core = me // 2, me % 2
    near, far, corner = half * 2 + 1 - core, (1 - half) * 2 + core, (1 - half) * 2 + 1 - core
    has_left, has_right = device > 0, device < dp_count - 1
    mesh_id = pl.DeviceIdType.MESH
    width = hidden_ref.shape[1]
    chunk = width // CHUNKS
    parts = []
    for array, source, later, from_left, from_right in (
        (hidden_ref, hidden_hbm, hidden_later, left_h, right_h),
        (query_ref, query_hbm, query_later, left_q, right_q),
        (upstream_ref, upstream_hbm, upstream_later, left_u, right_u),
    ):
        for at in range(0, array.shape[1], chunk):
            parts.append((array, later, from_left, from_right, slice(at, at + chunk), source))
    fetches = [
        pltpu.make_async_copy(source, target, local_done.at[n])
        for n, (source, target) in enumerate((
            (hidden_hbm, hidden_ref),
            (query_hbm, query_ref),
            (upstream_hbm, upstream_ref),
            (key_hbm, weight_ref.at[:, :HD]),
            (value_hbm, weight_ref.at[:, HD:]),
        ))
    ]

    def to_right(p):
        _, later, from_left, _, columns, _ = parts[p]
        return pltpu.make_async_remote_copy(
            src_ref=later.at[:, columns], dst_ref=from_left.at[:, columns],
            send_sem=right_sent.at[p], recv_sem=left_got.at[p],
            device_id={"dp": device + 1}, device_id_type=mesh_id,
        )

    def to_left(p):
        _, _, _, from_right, columns, source = parts[p]
        return pltpu.make_async_remote_copy(
            src_ref=source.at[:PIECE, columns], dst_ref=from_right.at[:, columns],
            send_sem=left_sent.at[p], recv_sem=right_got.at[p],
            device_id={"dp": device - 1}, device_id_type=mesh_id,
        )

    def over_mp(kind, c):
        owner, target = ((me, near), (me, far), (far, near))[kind]
        columns = slice(c * chunk, (c + 1) * chunk)
        return pltpu.make_async_remote_copy(
            src_ref=full.at[owner, :, columns], dst_ref=full.at[owner, :, columns],
            send_sem=mp_sent.at[kind, c], recv_sem=mp_got.at[kind, c],
            device_id={"mp": target}, device_id_type=mesh_id,
        )

    def settled(p):
        array, _, from_left, from_right, columns, _ = parts[p]

        @pl.when(has_left)
        def _():
            to_right(p).wait_recv()

        @pl.when(has_right)
        def _():
            to_left(p).wait_recv()

        own = PIECE + CAP_R
        total = jnp.dot(pick_ref[:, :PIECE], from_left[:, columns], preferred_element_type=jnp.float32)
        total += jnp.dot(pick_ref[:, PIECE:own], array[:, columns], preferred_element_type=jnp.float32)
        total += jnp.dot(pick_ref[:, own:], from_right[:, columns], preferred_element_type=jnp.float32)
        return total.astype(jnp.bfloat16)

    for fetch in fetches:
        fetch.start()
    barrier = pltpu.get_barrier_semaphore()
    for target in (near, far):
        pl.semaphore_signal(barrier, inc=1, device_id={"mp": target}, device_id_type=mesh_id)

    @pl.when(has_left)
    def _():
        pl.semaphore_signal(barrier, inc=1, device_id={"dp": device - 1}, device_id_type=mesh_id)

    @pl.when(has_right)
    def _():
        pl.semaphore_signal(barrier, inc=1, device_id={"dp": device + 1}, device_id_type=mesh_id)

    @pl.when(has_left & has_right)
    def _():
        pl.semaphore_wait(barrier, 4)

    @pl.when(jnp.logical_not(has_left & has_right))
    def _():
        pl.semaphore_wait(barrier, 3)

    def send(these):
        @pl.when(has_right)
        def _():
            for p in these:
                to_right(p).start()

        @pl.when(has_left)
        def _():
            for p in these:
                to_left(p).start()

    send(range(CHUNKS))

    @pl.when(jnp.logical_not(has_left))
    def _():
        for ref in (left_h, left_q, left_u):
            ref[...] = jnp.zeros_like(ref)

    @pl.when(jnp.logical_not(has_right))
    def _():
        for ref in (right_h, right_q, right_u):
            ref[...] = jnp.zeros_like(ref)

    fetches[0].wait()
    for c in range(CHUNKS):
        full[me, :, c * chunk : (c + 1) * chunk] = settled(c)
        send(range(CHUNKS + c, len(parts), CHUNKS))
        over_mp(1, c).start()
        over_mp(0, c).start()
        if c > 0:
            over_mp(1, c - 1).wait_recv()
            over_mp(2, c - 1).start()
    over_mp(1, CHUNKS - 1).wait_recv()
    over_mp(2, CHUNKS - 1).start()
    for c in range(CHUNKS):
        over_mp(0, c).wait_recv()
        over_mp(2, c).wait_recv()

    owners, rows, _ = full.shape
    tile = 256
    squares = jnp.zeros((rows, HD), jnp.float32)
    for owner in range(owners):
        for at in range(0, width, HD):
            wide = full[owner, :, at : at + HD].astype(jnp.float32)
            squares += wide * wide
    scale = lax.rsqrt(jnp.sum(squares, axis=1, keepdims=True) / (owners * width) + epsilon)
    for owner in range(owners):
        for at in range(0, width, tile):
            wide = full[owner, :, at : at + tile].astype(jnp.float32)
            spot = owner * width + at
            normed_ref[:, spot : spot + tile] = (wide * scale).astype(jnp.bfloat16)
    fetches[3].wait()
    fetches[4].wait()
    kv_ref[...] = jnp.dot(
        normed_ref[...], weight_ref[...], preferred_element_type=jnp.float32
    ).astype(jnp.bfloat16)
    fetches[1].wait()
    fetches[2].wait()
    for p in range(CHUNKS, len(parts)):
        target = query_out if parts[p][0] is query_ref else upstream_out
        target[:, parts[p][4]] = settled(p)

    @pl.when(has_right)
    def _():
        for p in range(len(parts)):
            to_right(p).wait_send()

    @pl.when(has_left)
    def _():
        for p in range(len(parts)):
            to_left(p).wait_send()

    for kind in range(3):
        for c in range(CHUNKS):
            over_mp(kind, c).wait_send()


def front(hidden, queries, upstream, key_weight, value_weight, own_piece, pick):
    width, head_width = hidden.shape[1], queries.shape[1]
    owners = lax.axis_size("mp")
    laters = [
        lax.dynamic_slice_in_dim(array, own_piece, PIECE, 0) for array in (hidden, queries, upstream)
    ]
    part_count = CHUNKS + 2 * (head_width * CHUNKS // width)
    vmem = pl.BlockSpec(memory_space=pltpu.VMEM)
    piece = lambda columns: pltpu.VMEM((PIECE, columns), jnp.bfloat16)
    part_sems = pltpu.SemaphoreType.DMA((part_count,))
    mp_sems = pltpu.SemaphoreType.DMA((3, CHUNKS))
    return pl.pallas_call(
        functools.partial(front_kernel, lax.axis_size("dp")),
        in_specs=[pl.BlockSpec(memory_space=pl.ANY)] * 5 + [vmem] * 4,
        out_specs=[vmem] * 4,
        out_shape=[
            jax.ShapeDtypeStruct((CAP_L, owners * width), jnp.bfloat16),
            jax.ShapeDtypeStruct((CAP_L, 2 * HD), jnp.bfloat16),
            jax.ShapeDtypeStruct((CAP_L, head_width), jnp.bfloat16),
            jax.ShapeDtypeStruct((CAP_L, head_width), jnp.bfloat16),
        ],
        scratch_shapes=[
            pltpu.VMEM(hidden.shape, jnp.bfloat16),
            pltpu.VMEM(queries.shape, jnp.bfloat16),
            pltpu.VMEM(upstream.shape, jnp.bfloat16),
            pltpu.VMEM((owners * width, 2 * HD), jnp.bfloat16),
            pltpu.SemaphoreType.DMA((5,)),
            pltpu.VMEM((owners, CAP_L, width), jnp.bfloat16),
            piece(width), piece(width),
            piece(head_width), piece(head_width),
            piece(head_width), piece(head_width),
            part_sems, part_sems, part_sems, part_sems, mp_sems, mp_sems,
        ],
        compiler_params=pltpu.CompilerParams(
            collective_id=1, has_side_effects=True, vmem_limit_bytes=48 * 1024 * 1024
        ),
    )(hidden, queries, upstream, key_weight, value_weight, *laters, pick)


def gradient_kernel(count, normed_ref, cots_ref, key_ref, value_ref, pair_out, pair_in, line_out,
                    line_in, acc, pair_sent, pair_got, line_sent, line_got):
    me = lax.axis_index("dp")
    lines = count // 2
    line, side = me // 2, me % 2
    width = acc.shape[2]
    mesh_id = pl.DeviceIdType.MESH

    def place(k):
        return (line + 1 + k) % lines

    def share(p, of_side):
        owner = place(p // 2) * 2 + of_side
        columns = pl.ds(pl.multiple_of(owner * width, width), width)
        rows = pl.ds(pl.multiple_of(p % 2 * HD, HD), HD)
        return jnp.dot(cots_ref[rows], normed_ref[:, columns], preferred_element_type=jnp.float32)

    def pair_copy(k):
        return pltpu.make_async_remote_copy(
            src_ref=pair_out.at[k], dst_ref=pair_in.at[k],
            send_sem=pair_sent.at[k], recv_sem=pair_got.at[k],
            device_id={"dp": line * 2 + 1 - side}, device_id_type=mesh_id,
        )

    def line_copy(k):
        return pltpu.make_async_remote_copy(
            src_ref=line_out.at[k], dst_ref=line_in.at[k],
            send_sem=line_sent.at[k], recv_sem=line_got.at[k],
            device_id={"dp": place(k // 2) * 2 + side}, device_id_type=mesh_id,
        )

    barrier = pltpu.get_barrier_semaphore()
    pl.semaphore_signal(barrier, inc=1, device_id={"dp": line * 2 + 1 - side}, device_id_type=mesh_id)

    @pl.loop(0, lines - 1)
    def _(k):
        pl.semaphore_signal(barrier, inc=1, device_id={"dp": place(k) * 2 + side}, device_id_type=mesh_id)

    pl.semaphore_wait(barrier, lines)
    total = 2 * lines

    for p in range(AHEAD):
        pair_out[p] = share(p, 1 - side).astype(jnp.bfloat16)
        pair_copy(p).start()

    @pl.loop(0, total - 2)
    def _(p):
        own = share(p, side)

        @pl.when(p + AHEAD < total)
        def _():
            pair_out[p + AHEAD] = share(p + AHEAD, 1 - side).astype(jnp.bfloat16)

        pair_copy(p).wait_recv()

        @pl.when(p + AHEAD < total)
        def _():
            pair_copy(p + AHEAD).start()

        line_out[p] = (own + pair_in[p].astype(jnp.float32)).astype(jnp.bfloat16)
        line_copy(p).start()

    for h in range(2):
        acc[h] = share(total - 2 + h, side)
    for h in range(2):
        pair_copy(total - 2 + h).wait_recv()
        acc[h] += pair_in[total - 2 + h].astype(jnp.float32)

    @pl.loop(0, lines - 1)
    def _(k):
        for h in range(2):
            line_copy(2 * k + h).wait_recv()
            acc[h] += line_in[2 * k + h].astype(jnp.float32)

    key_ref[...] = acc[0].T
    value_ref[...] = acc[1].T

    @pl.loop(0, total)
    def _(p):
        pair_copy(p).wait_send()

    @pl.loop(0, total - 2)
    def _(p):
        line_copy(p).wait_send()


def gradient_sum(normed, cots):
    count = lax.axis_size("dp")
    lines = count // 2
    width = normed.shape[1] // count
    vmem = pl.BlockSpec(memory_space=pltpu.VMEM)
    shares = lambda n: pltpu.VMEM((2 * n, HD, width), jnp.bfloat16)
    return pl.pallas_call(
        functools.partial(gradient_kernel, count),
        in_specs=[vmem, vmem],
        out_specs=[vmem, vmem],
        out_shape=[jax.ShapeDtypeStruct((width, HD), jnp.float32)] * 2,
        scratch_shapes=[
            shares(lines),
            shares(lines),
            shares(lines - 1),
            shares(lines - 1),
            pltpu.VMEM((2, HD, width), jnp.float32),
            pltpu.SemaphoreType.DMA((2 * lines,)),
            pltpu.SemaphoreType.DMA((2 * lines,)),
            pltpu.SemaphoreType.DMA((2 * lines - 2,)),
            pltpu.SemaphoreType.DMA((2 * lines - 2,)),
        ],
        compiler_params=pltpu.CompilerParams(
            collective_id=0, has_side_effects=True, vmem_limit_bytes=40 * 1024 * 1024
        ),
    )(normed, cots)


def body(hidden, queries, upstream, key_weight, value_weight, lengths, advantage):
    device = lax.axis_index("dp")
    segments, scales, source, own_piece = learner_rows(lengths, advantage, device)
    positions = jnp.arange(2 * PIECE + CAP_R, dtype=jnp.int32)
    pick = (source[:, None] == positions[None, :]).astype(jnp.bfloat16)

    normed, keys_values, query_rows, upstream_rows = front(
        hidden, queries, upstream, key_weight, value_weight, own_piece, pick
    )
    attention_out, cots = attend(query_rows, keys_values, upstream_rows, scales, segments)
    key_grad, value_grad = gradient_sum(normed, cots)
    return (attention_out, key_grad, value_grad)


def solution(mesh):
    in_specs = (P("dp", "mp"), P("dp", "mp"), P("dp", "mp"), P(None, "mp"), P(None, "mp"), P(), P())
    out_specs = (P("dp", "mp"), P("dp", "mp"), P("dp", "mp"))
    return jax.shard_map(body, mesh=mesh, in_specs=in_specs, out_specs=out_specs, check_vma=False)
```
